32 devices in a mesh: cell: 8 (over z, x), desc: 4 (over y, core).
Axes of the slice: x: 2, y: 2, z: 4, core: 2. Of those that a mesh axis runs over, the one named last changes fastest.
Arguments:
- cells: float32 [8192, 256], P('cell'), may hold values from -128 to 128
- descs: float32 [8192, 256], P('desc'), may hold values from -4 to 4
- g_start: float32 [8192], P('desc'), may hold values from -8 to 8
- cot_f: float32 [8192], P('cell'), may hold values from -24 to 24
- cot_g: float32 [8192], P('desc'), may hold values from -24 to 24
Outputs:
- grad_cells: float32 [8192, 256], P('cell')
- grad_descs: float32 [8192, 256], P('desc')
The draws below stay inside these ranges and needn't reach their ends.
All inputs are finite; a program needn't handle non-finite values.
Results may differ from the reference program's by a relative error of at most 0.0003.
Values sent between devices are 32-bit elements; how exact they have to be, the bound alone decides.
A program may use at most 192 MiB of HBM per device.

```python
import math
import jax
import jax.numpy as jnp
from jax import lax

W = 256
ITERS = 4
CELL_DEV = 1024
DESC_DEV = 2048
NC = 8192
ND = 8192
N_CELL = 8
N_DESC = 4


def shared_embeddings(key):
    key_x = jax.random.fold_in(key, 11)
    key_y = jax.random.fold_in(key, 12)
    key_noise = jax.random.fold_in(key, 13)
    key_strength = jax.random.fold_in(key, 14)
    total_cells = CELL_DEV * N_CELL
    total_desc = DESC_DEV * N_DESC
    col_ids = jnp.arange(total_desc)
    row_ids = jnp.arange(total_cells)
    noise = jnp.clip(jax.random.normal(key_noise, (total_desc, W), jnp.float32), -4.0, 4.0)
    paired = col_ids % 64 == 1
    yvals = jnp.clip(jax.random.normal(key_y, (total_desc, W), jnp.float32), -4.0, 4.0)
    xvals = jnp.clip(jax.random.normal(key_x, (total_cells, W), jnp.float32), -4.0, 4.0)
    xvals = xvals + 2.0
    before = jnp.roll(yvals, 1, axis=0)
    yvals = jnp.where(paired[:, None], before + 0.1 * math.sqrt(W) / 16.0 * noise, yvals)
    yvals = jnp.clip(yvals, -4.0, 4.0)
    starved = col_ids % 512 == 7
    yvals = jnp.where(starved[:, None], -4.0, yvals)
    planted = row_ids % 128 == 0
    target = row_ids // 128 * 64 % total_desc
    strength = (120.0 + 180.0 * jax.random.uniform(key_strength, (total_cells,), jnp.float32)) / (2.0 * math.sqrt(W))
    xvals = jnp.where(planted[:, None], strength[:, None] * jnp.take(yvals, target, axis=0), xvals)
    return (xvals, yvals)


def draw_cells(key, part):
    return shared_embeddings(key)[0].astype(jnp.float32)


def draw_descs(key, part):
    return shared_embeddings(key)[1].astype(jnp.float32)


def block_scale(rng, shape, split, least, largest):
    factor_of, own = 1.0, jax.random.fold_in(rng, 6)
    for dim, blocks in split:
        draws = jnp.exp(jax.random.uniform(jax.random.fold_in(own, dim), (blocks,), jnp.float32, least / len(split), largest / len(split)))
        factor_of = factor_of * jnp.repeat(draws, shape[dim] // blocks).reshape([-1 if axis == dim else 1 for axis in range(len(shape))])
    return factor_of


def bell_draw(stream_key, dims, scale, most, shards=(), dtype=jnp.bfloat16):
    entries = jax.random.normal(stream_key, dims, jnp.float32) * scale
    if len(shards) > 0:
        entries = block_scale(stream_key, dims, shards, -0.22, 0.18) * entries
    return jnp.clip(entries, min=-most, max=most).astype(dtype)


def setup_inputs(seed: int = 0) -> dict:
    splits = jax.random.split(jax.random.key(seed), 6)
    return {
        "cells": draw_cells(jax.random.fold_in(splits[5], 71), 0),
        "descs": draw_descs(jax.random.fold_in(splits[5], 71), 0),
        "g_start": bell_draw(splits[2], (ND,), 2.0, 8.0, ((0, 4),), jnp.float32),
        "cot_f": bell_draw(splits[3], (NC,), 4.0, 24.0, ((0, 8),), jnp.float32),
        "cot_g": bell_draw(splits[4], (ND,), 4.0, 24.0, ((0, 4),), jnp.float32),
    }


def reference(cells, descs, g_start, cot_f, cot_g):
    scale = 2.0 / math.sqrt(W)
    highest = lax.Precision.HIGHEST
    blocks = cells.reshape(N_CELL, CELL_DEV, W)
    cf_blocks = cot_f.reshape(N_CELL, CELL_DEV)
    total_desc = descs.shape[0]

    def logits(block):
        return lax.dot_general(block, descs, (((1,), (1,)), ((), ())), precision=highest, preferred_element_type=jnp.float32) * scale
    g_now = g_start
    f_list = []
    g_list = [g_start]
    for step in range(ITERS):

        def forward(carry, block):
            col_max, col_sum = carry
            lg = logits(block)
            zvals = lg + g_now[None, :]
            row_max = lax.optimization_barrier(jnp.max(zvals, axis=1))
            f_blk = -(row_max + jnp.log(lax.optimization_barrier(jnp.sum(jnp.exp(zvals - row_max[:, None]), axis=1))))
            wvals = lg + f_blk[:, None]
            new_max = jnp.maximum(col_max, lax.optimization_barrier(jnp.max(wvals, axis=0)))
            new_sum = col_sum * jnp.exp(col_max - new_max) + lax.optimization_barrier(jnp.sum(jnp.exp(wvals - new_max[None, :]), axis=0))
            return ((new_max, new_sum), f_blk)
        start = (jnp.full((total_desc,), -jnp.inf, jnp.float32), jnp.zeros((total_desc,), jnp.float32))
        (col_max, col_sum), f_blocks = lax.scan(forward, start, blocks)
        g_now = -(col_max + jnp.log(col_sum))
        f_list.append(f_blocks)
        g_list.append(g_now)
    gbar = cot_g
    grad_x = jnp.zeros((N_CELL, CELL_DEV, W), jnp.float32)
    grad_y = jnp.zeros((total_desc, W), jnp.float32)
    for step in reversed(range(ITERS)):
        g_here = g_list[step + 1]
        ratio = jnp.exp(g_list[step] - g_here)
        final = step == ITERS - 1
        gbar_now = gbar

        def backward(carry, item):
            gsum, gy = carry
            block, f_blk, cf_blk, gx_blk = item
            lg = logits(block)
            bplan = jnp.exp(lg + f_blk[:, None] + g_here[None, :])
            fbar = -lax.optimization_barrier(jnp.sum(bplan * gbar_now[None, :], axis=1))
            if final:
                fbar = fbar + cf_blk
            aplan = bplan * ratio[None, :]
            gsum = gsum - lax.optimization_barrier(jnp.sum(aplan * fbar[:, None], axis=0))
            lbar = -(bplan * gbar_now[None, :] + aplan * fbar[:, None])
            gx_blk = gx_blk + scale * jnp.dot(lbar, descs, precision=highest, preferred_element_type=jnp.float32)
            gy = gy + scale * lax.dot_general(lbar, block, (((0,), (0,)), ((), ())), precision=highest, preferred_element_type=jnp.float32)
            return ((gsum, gy), gx_blk)
        (gsum, grad_y), grad_x = lax.scan(backward, (jnp.zeros((total_desc,), jnp.float32), grad_y), (blocks, f_list[step], cf_blocks, grad_x))
        gbar = gsum
    return (grad_x.reshape(N_CELL * CELL_DEV, W), grad_y)
```

```python
import functools
import math

import jax
import jax.numpy as jnp
from jax import lax
from jax.experimental import pallas as pl
from jax.experimental.pallas import tpu as pltpu
from jax.sharding import PartitionSpec as P

ITERS = 4
MESH = pl.DeviceIdType.MESH
LANES = 128
F32 = jnp.float32
BF16 = jnp.bfloat16
LOG2E = math.log2(math.e)
CHUNKS = 4
PAIRS = ((0, 0), (0, 1), (1, 0), (0, 2), (2, 0), (1, 1))


def tree(op, parts):
    parts = list(parts)
    while len(parts) > 1:
        parts = [op(parts[i], parts[i + 1]) if i + 1 < len(parts) else parts[i] for i in range(0, len(parts), 2)]
    return parts[0]


def rotate(start, offset, count):
    return lax.rem(start + offset + count, count)


def split2(value):
    high = value.astype(BF16)
    return high, (value - high.astype(F32)).astype(BF16)


def split3(value):
    high = value.astype(BF16)
    rest = value - high.astype(F32)
    mid = rest.astype(BF16)
    return high, mid, (rest - mid.astype(F32)).astype(BF16)


def mm(a, b):
    return jnp.dot(a, b, preferred_element_type=F32)


def small_copy(axis, count, me, buf, send_sem, recv_sem, index, off):
    return pltpu.make_async_remote_copy(
        src_ref=buf.at[index, me],
        dst_ref=buf.at[index, me],
        send_sem=send_sem.at[index, off],
        recv_sem=recv_sem.at[index, me],
        device_id={axis: rotate(me, off, count)},
        device_id_type=MESH,
    )


def exchange(axis, count, me, buf, send_sem, recv_sem, index):
    for off in range(1, count):
        small_copy(axis, count, me, buf, send_sem, recv_sem, index, off).start()
    for off in range(1, count):
        source = rotate(me, -off, count)
        pltpu.make_async_remote_copy(
            src_ref=buf.at[index, source],
            dst_ref=buf.at[index, source],
            send_sem=send_sem.at[index, off],
            recv_sem=recv_sem.at[index, source],
            device_id={axis: rotate(me, off, count)},
            device_id_type=MESH,
        ).wait_recv()


def drain(axis, count, me, buf, send_sem, recv_sem, indices):
    for index in range(indices):
        for off in range(1, count):
            small_copy(axis, count, me, buf, send_sem, recv_sem, index, off).wait_send()


def combine(parts):
    top = tree(jnp.maximum, parts)
    return top + jnp.log(tree(jnp.add, [jnp.exp2(part - top) for part in parts])) * LOG2E


def plan_kernel(
    n_cell, n_desc,
    cells, descs, g_first, cf, cg,
    px, py,
    plan, vcol, racc_m, racc_s, cacc_m, cacc_s, wide,
    cat_c, cat_d, s_rows, t_rows, s_cat, t_cat,
    lb_high, lb_low, d_high, d_low, c_high, c_low,
    row_buf, col_buf, row_send, row_recv, col_send, col_recv,
    part_x, got_x, x_send, x_recv, part_y, got_y, y_send, y_recv,
):
    rows, width = cells.shape
    cols = descs.shape[0]
    scale = 2.0 / math.sqrt(width)
    my_cell = lax.axis_index("cell")
    my_desc = lax.axis_index("desc")
    blocks = cols // LANES
    x_block = rows // n_desc
    group = 16
    strips = 4

    barrier = pltpu.get_barrier_semaphore()
    for off in range(1, n_desc):
        pl.semaphore_signal(barrier, inc=1, device_id={"desc": rotate(my_desc, off, n_desc)}, device_id_type=MESH)
    for off in range(1, n_cell):
        pl.semaphore_signal(barrier, inc=1, device_id={"cell": rotate(my_cell, off, n_cell)}, device_id_type=MESH)

    def lane(b):
        return slice(b * LANES, (b + 1) * LANES)

    c_parts = split3(cells[...] * (scale * LOG2E))
    d_parts = split3(descs[...])
    for n, (i, j) in enumerate(PAIRS):
        cat_c[:, n * width:(n + 1) * width] = c_parts[i]
        cat_d[:, n * width:(n + 1) * width] = d_parts[j]
    d_high[...], d_low[...] = d_parts[0], d_parts[1]
    c_high[...], c_low[...] = split2(cells[...].T)

    def multiply(i, _):
        at = pl.ds(pl.multiple_of(i * 256, 256), 256)
        plan[at, :] = lax.dot_general(cat_c[at, :], cat_d[...], (((1,), (1,)), ((), ())), preferred_element_type=F32)
        return 0

    lax.fori_loop(0, rows // 256, multiply, 0)

    g_zero = g_first[...] * LOG2E
    wide[...] = jnp.broadcast_to(g_zero, (8, cols))

    def first_row(i, _):
        for u in range(strips):
            at = pl.ds(pl.multiple_of((i * strips + u) * 8, 8), 8)
            parts = [plan[at, lane(b)] + wide[:, lane(b)] for b in range(blocks)]
            top = tree(jnp.maximum, parts)
            racc_m[at, :] = top
            racc_s[at, :] = tree(jnp.add, [jnp.exp2(part - top) for part in parts])
        return 0

    lax.fori_loop(0, rows // (8 * strips), first_row, 0)
    tops = racc_m[...].T
    top = jnp.max(tops, axis=0, keepdims=True)
    total = jnp.sum(racc_s[...].T * jnp.exp2(tops - top), axis=0, keepdims=True)
    row_buf[0, my_desc] = top + jnp.log(total) * LOG2E
    pl.semaphore_wait(barrier, n_desc + n_cell - 2)
    exchange("desc", n_desc, my_desc, row_buf, row_send, row_recv, 0)
    f_one = -combine([row_buf[0, p] for p in range(n_desc)])

    def spread_rows(vector):
        vcol[...] = jnp.broadcast_to(vector, (LANES, rows)).T

    spread_rows(f_one)
    cacc_m[...] = jnp.full((8, cols), -jnp.inf, F32)
    cacc_s[...] = jnp.zeros((8, cols), F32)

    def first_col(i, _):
        base = i * (8 * group)
        for b in range(blocks):
            ats = [pl.ds(pl.multiple_of(base + 8 * u, 8), 8) for u in range(group)]
            parts = [plan[at, lane(b)] + vcol[at, :] for at in ats]
            before = cacc_m[:, lane(b)]
            top = jnp.maximum(before, tree(jnp.maximum, parts))
            cacc_m[:, lane(b)] = top
            cacc_s[:, lane(b)] = cacc_s[:, lane(b)] * jnp.exp2(before - top) + tree(
                jnp.add, [jnp.exp2(part - top) for part in parts]
            )
        return 0

    lax.fori_loop(0, rows // (8 * group), first_col, 0)
    top = jnp.max(cacc_m[...], axis=0, keepdims=True)
    total = jnp.sum(cacc_s[...] * jnp.exp2(cacc_m[...] - top), axis=0, keepdims=True)
    col_buf[0, my_cell] = top + jnp.log(total) * LOG2E
    exchange("cell", n_cell, my_cell, col_buf, col_send, col_recv, 0)
    g_one = -combine([col_buf[0, p] for p in range(n_cell)])
    wide[...] = jnp.broadcast_to(g_one, (8, cols))
    s_rows[0:1, :] = jnp.ones((1, rows), F32)
    t_rows[ITERS:ITERS + 1, :] = jnp.exp2(g_zero - g_one)
    t_rows[ITERS + 1:ITERS + 2, :] = jnp.ones((1, cols), F32)

    def make_plan(i, _):
        for u in range(strips):
            at = pl.ds(pl.multiple_of((i * strips + u) * 8, 8), 8)
            f_here = vcol[at, :]
            terms = []
            for b in range(blocks):
                value = jnp.exp2((plan[at, lane(b)] + f_here) + wide[:, lane(b)])
                plan[at, lane(b)] = value
                terms.append(value)
            racc_s[at, :] = tree(jnp.add, terms)
        return 0

    lax.fori_loop(0, rows // (8 * strips), make_plan, 0)

    def row_product():
        weights = [wide[:, lane(b)] for b in range(blocks)]

        def body(i, _):
            for u in range(strips):
                at = pl.ds(pl.multiple_of((i * strips + u) * 8, 8), 8)
                racc_s[at, :] = tree(jnp.add, [plan[at, lane(b)] * weights[b] for b in range(blocks)])
            return 0

        lax.fori_loop(0, rows // (8 * strips), body, 0)

    def row_sum(index):
        row_buf[index, my_desc] = jnp.sum(racc_s[...].T, axis=0, keepdims=True)
        exchange("desc", n_desc, my_desc, row_buf, row_send, row_recv, index)
        return tree(jnp.add, [row_buf[index, p] for p in range(n_desc)])

    def col_sum(index):
        def body(i, totals):
            for u in range(strips):
                at = pl.ds(pl.multiple_of((i * strips + u) * 8, 8), 8)
                here = vcol[at, :]
                totals = [totals[b] + plan[at, lane(b)] * here for b in range(blocks)]
            return totals

        totals = lax.fori_loop(0, rows // (8 * strips), body, [jnp.zeros((8, LANES), F32)] * blocks)
        for b in range(blocks):
            col_buf[index, my_cell, :, lane(b)] = jnp.sum(totals[b], axis=0, keepdims=True)
        exchange("cell", n_cell, my_cell, col_buf, col_send, col_recv, index)
        return tree(jnp.add, [col_buf[index, p] for p in range(n_cell)])

    def forward(k, w_last):
        u_now = 1.0 / row_sum(k)
        s_rows[pl.ds(k, 1), :] = u_now
        spread_rows(u_now)
        w_now = 1.0 / col_sum(k)

        @pl.when(k < ITERS - 1)
        def _():
            t_rows[pl.ds(ITERS + 1 + k, 1), :] = w_now
            wide[...] = jnp.broadcast_to(w_now, (8, cols))
            row_product()

        return w_now

    w_last = lax.fori_loop(1, ITERS, forward, jnp.ones((1, cols), F32))

    def backward(t, a_now):
        k = ITERS - 1 - t
        t_rows[pl.ds(k, 1), :] = a_now
        wide[...] = jnp.broadcast_to(a_now, (8, cols))
        row_product()
        u_now = s_rows[pl.ds(k, 1), :]
        fbar = -(u_now * row_sum(ITERS + t)) + jnp.where(t == 0, cf[...], 0.0)
        b_now = u_now * fbar
        s_rows[pl.ds(ITERS + k, 1), :] = b_now

        def more(_):
            spread_rows(b_now)
            w_before = t_rows[pl.ds(ITERS + k, 1), :]
            return -(w_before * w_before * col_sum(ITERS + t))

        return lax.cond(t < ITERS - 1, more, lambda _: a_now, 0)

    lax.fori_loop(0, ITERS, backward, w_last * cg[...])

    s_parts = [part.astype(F32) for part in split3(s_rows[...])]
    t_parts = [part.astype(F32) for part in split3(t_rows[...])]
    pad = LANES - 2 * ITERS * len(PAIRS)
    s_all = jnp.concatenate([s_parts[i] for i, _ in PAIRS] + [jnp.zeros((pad, rows), F32)], axis=0)
    t_all = jnp.concatenate([t_parts[j] for _, j in PAIRS] + [jnp.zeros((pad, cols), F32)], axis=0)
    s_cat[...] = s_all.T.astype(BF16)
    t_cat[...] = t_all.astype(BF16)

    y_chunk = cols // CHUNKS
    levels = n_cell.bit_length() - 1
    orders = [list(range(levels)), list(range(1, levels)) + [0]]

    def y_plan(chunk):
        steps, start, size, place = [], chunk * y_chunk, y_chunk, 0
        for bit in orders[chunk % 2]:
            mine = lax.rem(my_cell // (1 << bit), 2)
            peer = my_cell + (1 - 2 * mine) * (1 << bit)
            size = size // 2
            sent = start + (1 - mine) * size
            start = start + mine * size
            steps.append((peer, pl.multiple_of(sent, 8), pl.multiple_of(start, 8), size, place))
            place += size
        return steps

    def y_scatter(chunk, level, step):
        peer, sent, kept, size, place = step
        return pltpu.make_async_remote_copy(
            src_ref=part_y.at[pl.ds(sent, size)],
            dst_ref=got_y.at[chunk, pl.ds(place, size)],
            send_sem=y_send.at[0, chunk, level],
            recv_sem=y_recv.at[0, chunk, level],
            device_id={"cell": peer},
            device_id_type=MESH,
        )

    def y_gather(chunk, level, step, arriving=False):
        peer, sent, kept, size, place = step
        at = pl.ds(sent if arriving else kept, size)
        return pltpu.make_async_remote_copy(
            src_ref=py.at[at],
            dst_ref=py.at[at],
            send_sem=y_send.at[1, chunk, level],
            recv_sem=y_recv.at[1, chunk, level],
            device_id={"cell": peer},
            device_id_type=MESH,
        )

    plans = [y_plan(chunk) for chunk in range(CHUNKS)]

    def y_add(chunk, level):
        peer, sent, kept, size, place = plans[chunk][level]
        y_scatter(chunk, level, plans[chunk][level]).wait_recv()
        out = part_y if level + 1 < levels else py
        out[pl.ds(kept, size), :] = part_y[pl.ds(kept, size), :] + got_y[chunk, pl.ds(place, size), :]
        if level + 1 < levels:
            y_scatter(chunk, level + 1, plans[chunk][level + 1]).start()
        else:
            y_gather(chunk, level, plans[chunk][level]).start()

    def y_spread(chunk, level):
        y_gather(chunk, level, plans[chunk][level], True).wait_recv()
        if level > 0:
            y_gather(chunk, level - 1, plans[chunk][level - 1]).start()

    for chunk in range(CHUNKS):
        def y_tile(i, _):
            at = pl.ds(pl.multiple_of(chunk * y_chunk + i * 256, 256), 256)
            high, low = split2(plan[:, at] * mm(s_cat[...], t_cat[:, at]))
            lb_high[:, at], lb_low[:, at] = high, low
            part_y[at, :] = (-scale) * (mm(c_high[...], high) + (mm(c_low[...], high) + mm(c_high[...], low))).T
            return 0

        lax.fori_loop(0, y_chunk // 256, y_tile, 0)
        y_scatter(chunk, 0, plans[chunk][0]).start()

    def x_tile(owner):
        at = pl.ds(pl.multiple_of(owner * x_block, x_block), x_block)
        high, low = lb_high[at, :], lb_low[at, :]
        return (-scale) * (mm(high, d_high[...]) + (mm(low, d_high[...]) + mm(high, d_low[...])))

    def x_scatter(off, peer, slot):
        return pltpu.make_async_remote_copy(
            src_ref=part_x.at[peer],
            dst_ref=got_x.at[slot],
            send_sem=x_send.at[0, off],
            recv_sem=x_recv.at[0, slot],
            device_id={"desc": peer},
            device_id_type=MESH,
        )

    def x_gather(off, peer, slot):
        at = pl.ds(pl.multiple_of(slot * x_block, x_block), x_block)
        return pltpu.make_async_remote_copy(
            src_ref=px.at[at],
            dst_ref=px.at[at],
            send_sem=x_send.at[1, off],
            recv_sem=x_recv.at[1, slot],
            device_id={"desc": peer},
            device_id_type=MESH,
        )

    def send_x(off, _):
        owner = rotate(my_desc, off, n_desc)
        part_x[owner] = x_tile(owner)
        x_scatter(off, owner, my_desc).start()
        return 0

    lax.fori_loop(1, n_desc, send_x, 0)
    got_x[my_desc] = x_tile(my_desc)

    for level in range(levels):
        for chunk in range(CHUNKS):
            y_add(chunk, level)
        if level == 0:
            for off in range(1, n_desc):
                x_scatter(off, rotate(my_desc, off, n_desc), rotate(my_desc, -off, n_desc)).wait_recv()
            my_rows = pl.ds(pl.multiple_of(my_desc * x_block, x_block), x_block)
            px[my_rows, :] = tree(jnp.add, [got_x[p] for p in range(n_desc)])
            for off in range(1, n_desc):
                x_gather(off, rotate(my_desc, off, n_desc), my_desc).start()
    for level in reversed(range(levels)):
        for chunk in range(CHUNKS):
            y_spread(chunk, level)

    for off in range(1, n_desc):
        peer, source = rotate(my_desc, off, n_desc), rotate(my_desc, -off, n_desc)
        x_gather(off, peer, source).wait_recv()
        x_scatter(off, peer, source).wait_send()
        x_gather(off, peer, my_desc).wait_send()
    for chunk in range(CHUNKS):
        for level in range(levels):
            y_scatter(chunk, level, plans[chunk][level]).wait_send()
            y_gather(chunk, level, plans[chunk][level]).wait_send()
    drain("desc", n_desc, my_desc, row_buf, row_send, row_recv, 2 * ITERS)
    drain("cell", n_cell, my_cell, col_buf, col_send, col_recv, 2 * ITERS - 1)


def run_plan(n_cell, n_desc, cells, descs, g_start, cot_f, cot_g):
    rows, width = cells.shape
    cols = descs.shape[0]
    vmem = pltpu.VMEM
    dma = pltpu.SemaphoreType.DMA
    spec = pl.BlockSpec(memory_space=pltpu.VMEM)
    n_row, n_col = 2 * ITERS, 2 * ITERS - 1
    levels = n_cell.bit_length() - 1
    return pl.pallas_call(
        functools.partial(plan_kernel, n_cell, n_desc),
        out_shape=(
            jax.ShapeDtypeStruct((rows, width), F32),
            jax.ShapeDtypeStruct((cols, width), F32),
        ),
        in_specs=[spec] * 5,
        out_specs=(spec, spec),
        scratch_shapes=[
            vmem((rows, cols), F32),
            vmem((rows, LANES), F32),
            vmem((rows, LANES), F32),
            vmem((rows, LANES), F32),
            vmem((8, cols), F32),
            vmem((8, cols), F32),
            vmem((8, cols), F32),
            vmem((rows, len(PAIRS) * width), BF16),
            vmem((cols, len(PAIRS) * width), BF16),
            vmem((2 * ITERS, rows), F32),
            vmem((2 * ITERS, cols), F32),
            vmem((rows, LANES), BF16),
            vmem((LANES, cols), BF16),
            vmem((rows, cols), BF16),
            vmem((rows, cols), BF16),
            vmem((cols, width), BF16),
            vmem((cols, width), BF16),
            vmem((width, rows), BF16),
            vmem((width, rows), BF16),
            vmem((n_row, n_desc, 1, rows), F32),
            vmem((n_col, n_cell, 1, cols), F32),
            dma((n_row, n_desc)),
            dma((n_row, n_desc)),
            dma((n_col, n_cell)),
            dma((n_col, n_cell)),
            vmem((n_desc, rows // n_desc, width), F32),
            vmem((n_desc, rows // n_desc, width), F32),
            dma((2, n_desc)),
            dma((2, n_desc)),
            vmem((cols, width), F32),
            vmem((CHUNKS, cols // CHUNKS, width), F32),
            dma((2, CHUNKS, levels)),
            dma((2, CHUNKS, levels)),
        ],
        compiler_params=pltpu.CompilerParams(
            collective_id=0, has_side_effects=True, vmem_limit_bytes=60 * 1024 * 1024
        ),
        name="plan",
    )(cells, descs, g_start[None, :], cot_f[None, :], cot_g[None, :])


def solution(mesh):
    n_cell = mesh.shape["cell"]
    n_desc = mesh.shape["desc"]

    def on_device(cells, descs, g_start, cot_f, cot_g):
        return run_plan(n_cell, n_desc, cells, descs, g_start, cot_f, cot_g)

    placed = (P("cell", None), P("desc", None), P("desc"), P("cell"), P("desc"))
    return jax.shard_map(
        on_device,
        mesh=mesh,
        in_specs=placed,
        out_specs=(P("cell", None), P("desc", None)),
        check_vma=False,
    )
```

```python
import functools
import math

import jax
import jax.numpy as jnp
from jax import lax
from jax.experimental import pallas as pl
from jax.experimental.pallas import tpu as pltpu
from jax.sharding import PartitionSpec as P

ITERS = 4
MESH = pl.DeviceIdType.MESH
LANES = 128
F32 = jnp.float32
BF16 = jnp.bfloat16
LOG2E = math.log2(math.e)
X_CHUNKS = 2
Y_CHUNKS = 4
PIECES = 4
PAIRS = ((0, 0), (0, 1), (1, 0), (0, 2), (2, 0), (1, 1))


def tree(op, parts):
    parts = list(parts)
    while len(parts) > 1:
        parts = [op(parts[i], parts[i + 1]) if i + 1 < len(parts) else parts[i] for i in range(0, len(parts), 2)]
    return parts[0]


def rotate(start, offset, count):
    return lax.rem(start + offset + count, count)


def split2(value):
    high = value.astype(BF16)
    return high, (value - high.astype(F32)).astype(BF16)


def split3(value):
    high = value.astype(BF16)
    rest = value - high.astype(F32)
    mid = rest.astype(BF16)
    return high, mid, (rest - mid.astype(F32)).astype(BF16)


def mm(a, b):
    return jnp.dot(a, b, preferred_element_type=F32)


def small_copy(axis, count, me, buf, send_sem, recv_sem, index, off):
    return pltpu.make_async_remote_copy(
        src_ref=buf.at[index, me],
        dst_ref=buf.at[index, me],
        send_sem=send_sem.at[index, off],
        recv_sem=recv_sem.at[index, me],
        device_id={axis: rotate(me, off, count)},
        device_id_type=MESH,
    )


def exchange(axis, count, me, buf, send_sem, recv_sem, index, between):
    for off in range(1, count):
        small_copy(axis, count, me, buf, send_sem, recv_sem, index, off).start()
    between()
    for off in range(1, count):
        source = rotate(me, -off, count)
        pltpu.make_async_remote_copy(
            src_ref=buf.at[index, source],
            dst_ref=buf.at[index, source],
            send_sem=send_sem.at[index, off],
            recv_sem=recv_sem.at[index, source],
            device_id={axis: rotate(me, off, count)},
            device_id_type=MESH,
        ).wait_recv()


def flip(index, bits):
    for bit in range(bits.bit_length()):
        if bits >> bit & 1:
            index = index + (1 - 2 * lax.rem(index // (1 << bit), 2)) * (1 << bit)
    return index


def last_hop(rel):
    return rel & -rel


def bulk_schedule(count, pieces, windows):
    top = count // 2
    limit = 3
    while True:
        came = {(p, 0): -1 for p in range(pieces)}
        plan = []
        for window in range(windows):
            left = {1 << b: limit + (window == 0) for b in range(count.bit_length() - 1)}
            sent = []
            for hop in sorted(left, reverse=True):
                for (p, rel), when in sorted(came.items(), key=lambda item: (item[1], item[0])):
                    to = rel | hop
                    if when >= window or (p, to) in came or last_hop(to) != hop or rel & hop:
                        continue
                    cost = 2 if hop == top else 1
                    if left[hop] < cost:
                        continue
                    left[hop] -= cost
                    if hop == top and top > 1:
                        left[top // 2] -= 1
                    came[p, to] = window
                    sent.append((p, to))
            plan.append(sent)
        if len(came) == pieces * count:
            return plan
        limit += 1


def drain(axis, count, me, buf, send_sem, recv_sem, indices):
    for index in range(indices):
        for off in range(1, count):
            small_copy(axis, count, me, buf, send_sem, recv_sem, index, off).wait_send()


def combine(parts):
    top = tree(jnp.maximum, parts)
    return top + jnp.log(tree(jnp.add, [jnp.exp2(part - top) for part in parts])) * LOG2E


def plan_kernel(
    n_cell, n_desc,
    cells, descs, g_first, cf, cg,
    px, py,
    plan, vcol, racc_m, racc_s, cacc_m, cacc_s, wide,
    cat_c, cat_d, s_rows, t_rows, g_row, s_cat, t_cat,
    row_buf, col_buf, row_send, row_recv, col_send, col_recv,
    part_x, got_x, x_send, x_recv,
    far_cells, far_send, far_recv, swap_send, swap_recv,
    vec_buf, vec_send, vec_recv,
    slab, g_slab, cat_t, keep_h, keep_m, sum_y, y_send, y_recv,
):
    rows, width = cells.shape
    cols = descs.shape[0]
    scale = 2.0 / math.sqrt(width)
    my_cell = lax.axis_index("cell")
    my_desc = lax.axis_index("desc")
    side = lax.rem(my_desc, 2)
    blocks = cols // LANES
    y_block = cols // n_cell
    half = rows // 2
    piece = half // PIECES
    group = 16
    strips = 4
    keep = keep_h.shape[0] == n_cell * rows

    barrier = pltpu.get_barrier_semaphore()
    for off in range(1, n_desc):
        pl.semaphore_signal(barrier, inc=1, device_id={"desc": rotate(my_desc, off, n_desc)}, device_id_type=MESH)
    for off in range(1, n_cell):
        pl.semaphore_signal(barrier, inc=1, device_id={"cell": rotate(my_cell, off, n_cell)}, device_id_type=MESH)

    def lane(b):
        return slice(b * LANES, (b + 1) * LANES)

    def fill(cat, value, which):
        parts = split3(value)
        for n, pair in enumerate(PAIRS):
            cat[:, n * width:(n + 1) * width] = parts[pair[which]]
        return parts

    def contract(a, b):
        return lax.dot_general(a, b, (((1,), (1,)), ((), ())), preferred_element_type=F32)

    fill(cat_c, cells[...] * (scale * LOG2E), 0)
    fill(cat_d, descs[...], 1)

    def multiply(i, _):
        at = pl.ds(pl.multiple_of(i * 256, 256), 256)
        plan[at, :] = contract(cat_c[at, :], cat_d[...])
        return 0

    lax.fori_loop(0, rows // 256, multiply, 0)
    g_zero = g_first[...] * LOG2E
    wide[...] = jnp.broadcast_to(g_zero, (8, cols))
    pl.semaphore_wait(barrier, n_desc + n_cell - 2)

    schedule = bulk_schedule(n_cell, PIECES, 2 * ITERS - 1)

    def far_rows(p, which):
        return pl.ds(pl.multiple_of(which * half + p * piece, piece), piece)

    def far_copy(p, rel):
        hop = last_hop(rel)
        at = far_rows(p, side)
        return pltpu.make_async_remote_copy(
            src_ref=cells.at[at] if rel == hop else far_cells.at[rel ^ hop, at],
            dst_ref=far_cells.at[rel, at],
            send_sem=far_send.at[p, rel],
            recv_sem=far_recv.at[p, rel],
            device_id={"cell": flip(my_cell, hop)},
            device_id_type=MESH,
        )

    def swap_copy(p, rel, which):
        at = far_rows(p, which)
        return pltpu.make_async_remote_copy(
            src_ref=far_cells.at[rel, at],
            dst_ref=far_cells.at[rel, at],
            send_sem=swap_send.at[p, rel],
            recv_sem=swap_recv.at[p, rel],
            device_id={"desc": flip(my_desc, 1)},
            device_id_type=MESH,
        )

    def vec_copy(v, rel):
        return pltpu.make_async_remote_copy(
            src_ref=vec_buf.at[v, 0],
            dst_ref=vec_buf.at[v, rel],
            send_sem=vec_send.at[v, rel],
            recv_sem=vec_recv.at[v, rel],
            device_id={"cell": flip(my_cell, rel)},
            device_id_type=MESH,
        )

    def send_vec(v):
        for rel in range(1, n_cell):
            vec_copy(v, rel).start()

    my_slab = pl.ds(pl.multiple_of(my_cell * y_block, y_block), y_block)

    def slab_task(rel, which):
        start = pl.multiple_of(which * half, half)
        at = pl.ds(start, half)
        source = cells[at, :] if rel == 0 else far_cells[rel, at, :]
        parts = fill(cat_t, source * (scale * LOG2E), 0)
        if keep:
            put = pl.ds(pl.multiple_of(rel * rows + start, half), half)
            keep_h[put, :], keep_m[put, :] = parts[0], parts[1]
        logits = contract(cat_d[my_slab, :], cat_t[...])
        out = pl.ds(pl.multiple_of(rel * rows + start, half), half)
        g_here = jnp.concatenate([g_slab[...]] * (half // LANES), axis=1)
        slab[:, out] = jnp.exp2((logits + vec_buf[0, rel, :, at]) + g_here)

    tasks = [(0, side), (0, 1 - side)]
    seen = {}
    swapping = []
    ready = {0}

    def run_tasks(most):
        for _ in range(min(most, len(tasks))):
            rel, which = tasks.pop(0)
            if rel not in ready:
                vec_copy(0, rel).wait_recv()
                ready.add(rel)
            slab_task(rel, which)

    def window(w):
        arrived = schedule[w - 1] if 0 < w <= len(schedule) else []
        for p, rel in arrived:
            far_copy(p, rel).wait_recv()
        for p, rel in schedule[w] if w < len(schedule) else []:
            far_copy(p, rel).start()
        for p, rel in arrived:
            swap_copy(p, rel, side).start()
            swapping.append((p, rel))
            seen[rel] = seen.get(rel, 0) + 1
            if seen[rel] == PIECES:
                tasks.append((rel, side))

    def finish_swaps():
        for p, rel in swapping:
            swap_copy(p, rel, 1 - side).wait_recv()
            seen[rel, 1] = seen.get((rel, 1), 0) + 1
            if seen[rel, 1] == PIECES:
                tasks.append((rel, 1 - side))
        swapping.clear()

    window(0)

    def first_row(i, _):
        for u in range(strips):
            at = pl.ds(pl.multiple_of((i * strips + u) * 8, 8), 8)
            parts = [plan[at, lane(b)] + wide[:, lane(b)] for b in range(blocks)]
            top = tree(jnp.maximum, parts)
            racc_m[at, :] = top
            racc_s[at, :] = tree(jnp.add, [jnp.exp2(part - top) for part in parts])
        return 0

    lax.fori_loop(0, rows // (8 * strips), first_row, 0)
    tops = racc_m[...].T
    top = jnp.max(tops, axis=0, keepdims=True)
    total = jnp.sum(racc_s[...].T * jnp.exp2(tops - top), axis=0, keepdims=True)
    row_buf[0, my_desc] = top + jnp.log(total) * LOG2E
    exchange("desc", n_desc, my_desc, row_buf, row_send, row_recv, 0, lambda: None)
    f_one = -combine([row_buf[0, p] for p in range(n_desc)])
    vec_buf[0, 0] = f_one

    def spread_rows(vector):
        vcol[...] = jnp.broadcast_to(vector, (LANES, rows)).T

    spread_rows(f_one)
    cacc_m[...] = jnp.full((8, cols), -jnp.inf, F32)
    cacc_s[...] = jnp.zeros((8, cols), F32)

    def first_col(i, _):
        base = i * (8 * group)
        for b in range(blocks):
            ats = [pl.ds(pl.multiple_of(base + 8 * u, 8), 8) for u in range(group)]
            parts = [plan[at, lane(b)] + vcol[at, :] for at in ats]
            before = cacc_m[:, lane(b)]
            top = jnp.maximum(before, tree(jnp.maximum, parts))
            cacc_m[:, lane(b)] = top
            cacc_s[:, lane(b)] = cacc_s[:, lane(b)] * jnp.exp2(before - top) + tree(
                jnp.add, [jnp.exp2(part - top) for part in parts]
            )
        return 0

    lax.fori_loop(0, rows // (8 * group), first_col, 0)
    top = jnp.max(cacc_m[...], axis=0, keepdims=True)
    total = jnp.sum(cacc_s[...] * jnp.exp2(cacc_m[...] - top), axis=0, keepdims=True)
    col_buf[0, my_cell] = top + jnp.log(total) * LOG2E

    def after_first():
        send_vec(0)
        window(1)

    exchange("cell", n_cell, my_cell, col_buf, col_send, col_recv, 0, after_first)
    g_one = -combine([col_buf[0, p] for p in range(n_cell)])
    wide[...] = jnp.broadcast_to(g_one, (8, cols))
    g_row[...] = g_one
    g_slab[...] = jnp.broadcast_to(g_row[:, my_slab], (LANES, y_block)).T
    s_rows[0:1, :] = jnp.ones((1, rows), F32)
    t_rows[ITERS:ITERS + 1, :] = jnp.exp2(g_zero - g_one)
    t_rows[ITERS + 1:ITERS + 2, :] = jnp.ones((1, cols), F32)

    def make_plan(i, _):
        for u in range(strips):
            at = pl.ds(pl.multiple_of((i * strips + u) * 8, 8), 8)
            f_here = vcol[at, :]
            terms = []
            for b in range(blocks):
                value = jnp.exp2((plan[at, lane(b)] + f_here) + wide[:, lane(b)])
                plan[at, lane(b)] = value
                terms.append(value)
            racc_s[at, :] = tree(jnp.add, terms)
        return 0

    lax.fori_loop(0, rows // (8 * strips), make_plan, 0)

    def row_product(weight):
        wide[...] = jnp.broadcast_to(weight, (8, cols))
        weights = [wide[:, lane(b)] for b in range(blocks)]

        def body(i, _):
            for u in range(strips):
                at = pl.ds(pl.multiple_of((i * strips + u) * 8, 8), 8)
                racc_s[at, :] = tree(jnp.add, [plan[at, lane(b)] * weights[b] for b in range(blocks)])
            return 0

        lax.fori_loop(0, rows // (8 * strips), body, 0)

    def row_sum(index, most):
        def between():
            finish_swaps()
            run_tasks(most)

        row_buf[index, my_desc] = jnp.sum(racc_s[...].T, axis=0, keepdims=True)
        exchange("desc", n_desc, my_desc, row_buf, row_send, row_recv, index, between)
        return tree(jnp.add, [row_buf[index, p] for p in range(n_desc)])

    def col_sum(vector, v, index, w):
        def between():
            send_vec(v)
            window(w)
            run_tasks(3)

        def body(i, totals):
            for u in range(strips):
                at = pl.ds(pl.multiple_of((i * strips + u) * 8, 8), 8)
                here = vcol[at, :]
                totals = [totals[b] + plan[at, lane(b)] * here for b in range(blocks)]
            return totals

        vec_buf[v, 0] = vector
        spread_rows(vector)
        totals = lax.fori_loop(0, rows // (8 * strips), body, [jnp.zeros((8, LANES), F32)] * blocks)
        for b in range(blocks):
            col_buf[index, my_cell, :, lane(b)] = jnp.sum(totals[b], axis=0, keepdims=True)
        exchange("cell", n_cell, my_cell, col_buf, col_send, col_recv, index, between)
        return tree(jnp.add, [col_buf[index, p] for p in range(n_cell)])

    for k in range(1, ITERS):
        u_now = 1.0 / row_sum(k, 2)
        s_rows[k:k + 1, :] = u_now
        w_now = 1.0 / col_sum(u_now, k, k, k + 1)
        if k < ITERS - 1:
            t_rows[ITERS + 1 + k:ITERS + 2 + k, :] = w_now
            row_product(w_now)

    a_now = w_now * cg[...]
    for k in reversed(range(ITERS)):
        t = ITERS - 1 - k
        t_rows[k:k + 1, :] = a_now
        row_product(a_now)
        u_now = s_rows[k:k + 1, :]
        fbar = -(u_now * row_sum(ITERS + t, 2 if k > 0 else len(tasks) + 2 * n_cell))
        if k == ITERS - 1:
            fbar = fbar + cf[...]
        b_now = u_now * fbar
        s_rows[ITERS + k:ITERS + k + 1, :] = b_now
        if k > 0:
            w_before = t_rows[ITERS + k:ITERS + k + 1, :]
            a_now = -(w_before * (w_before * col_sum(b_now, ITERS + k, ITERS + t, ITERS + 1 + t)))
        else:
            vec_buf[ITERS, 0] = b_now
            send_vec(ITERS)

    pad = LANES - 2 * ITERS * len(PAIRS)

    def stack(value, which):
        parts = [part.astype(F32) for part in split3(value)]
        return jnp.concatenate([parts[pair[which]] for pair in PAIRS] + [jnp.zeros((pad, value.shape[1]), F32)], axis=0)

    s_cat[...] = stack(s_rows[...], 0).T.astype(BF16)
    t_cat[...] = stack(t_rows[...], 1).astype(BF16)

    x_chunk = rows // X_CHUNKS
    levels = n_desc.bit_length() - 1

    def x_plan(chunk):
        steps, start, size, place = [], chunk * x_chunk, x_chunk, chunk * x_chunk
        for bit in range(levels):
            mine = lax.rem(my_desc // (1 << bit), 2)
            size = size // 2
            sent = start + (1 - mine) * size
            start = start + mine * size
            steps.append((flip(my_desc, 1 << bit), pl.multiple_of(sent, 8), pl.multiple_of(start, 8), size, place))
            place += size
        return steps

    plans = [x_plan(chunk) for chunk in range(X_CHUNKS)]

    def x_scatter(chunk, level):
        peer, sent, kept, size, place = plans[chunk][level]
        return pltpu.make_async_remote_copy(
            src_ref=part_x.at[pl.ds(sent, size)],
            dst_ref=got_x.at[pl.ds(place, size)],
            send_sem=x_send.at[0, chunk, level],
            recv_sem=x_recv.at[0, chunk, level],
            device_id={"desc": peer},
            device_id_type=MESH,
        )

    def x_gather(chunk, level, arriving=False):
        peer, sent, kept, size, place = plans[chunk][level]
        at = pl.ds(sent if arriving else kept, size)
        return pltpu.make_async_remote_copy(
            src_ref=px.at[at],
            dst_ref=px.at[at],
            send_sem=x_send.at[1, chunk, level],
            recv_sem=x_recv.at[1, chunk, level],
            device_id={"desc": peer},
            device_id_type=MESH,
        )

    def x_add(chunk, level):
        peer, sent, kept, size, place = plans[chunk][level]
        x_scatter(chunk, level).wait_recv()
        out = part_x if level + 1 < levels else px
        out[pl.ds(kept, size), :] = part_x[pl.ds(kept, size), :] + got_x[pl.ds(place, size), :]
        if level + 1 < levels:
            x_scatter(chunk, level + 1).start()
        else:
            x_gather(chunk, level).start()

    def x_spread(chunk, level):
        x_gather(chunk, level, True).wait_recv()
        if level > 0:
            x_gather(chunk, level - 1).start()

    def x_tile(at):
        high, low = split2(plan[at, :] * mm(s_cat[at, :], t_cat[...]))
        d_high, d_low = cat_d[:, :width], cat_d[:, width:2 * width]
        part_x[at, :] = (-scale) * (mm(high, d_high) + (mm(low, d_high) + mm(high, d_low)))

    for chunk in range(X_CHUNKS):
        for first in (True, False):
            peer, sent, kept, size, place = plans[chunk][0]
            x_tile(pl.ds(sent if first else kept, size))
            if first:
                x_scatter(chunk, 0).start()

    for level in range(levels):
        for chunk in range(X_CHUNKS):
            x_add(chunk, level)

    for v in range(1, 2 * ITERS):
        for rel in range(1, n_cell):
            vec_copy(v, rel).wait_recv()
    t_part = stack(t_rows[:, my_slab], 1).T.astype(BF16)
    sum_y[...] = jnp.zeros((y_block, width), F32)

    def y_step(rel, _):
        at = pl.ds(pl.multiple_of(rel * rows, rows), rows)
        s_here = jnp.concatenate(
            [jnp.ones((1, rows), F32)] + [vec_buf[v, rel] for v in range(1, 2 * ITERS)], axis=0
        )
        high, low = split2(slab[:, at] * mm(t_part, stack(s_here, 0).astype(BF16)))
        if keep:
            c_high, c_mid = keep_h[at, :], keep_m[at, :]
        else:
            c_high, c_mid = split2(far_cells[rel] * (scale * LOG2E))
        sum_y[...] = sum_y[...] + (mm(high, c_high) + (mm(low, c_high) + mm(high, c_mid)))
        return 0

    if not keep:
        far_cells[0] = cells[...]
    lax.fori_loop(0, n_cell, y_step, 0)
    py[my_slab, :] = sum_y[...] * (-1.0 / LOG2E)

    y_rows = y_block // Y_CHUNKS

    def y_copy(chunk, rel, arriving=False):
        hop = last_hop(rel)
        owner = flip(my_cell, rel if arriving else rel ^ hop)
        at = pl.ds(pl.multiple_of(owner * y_block + chunk * y_rows, y_rows), y_rows)
        return pltpu.make_async_remote_copy(
            src_ref=py.at[at],
            dst_ref=py.at[at],
            send_sem=y_send.at[chunk, rel],
            recv_sem=y_recv.at[chunk, rel],
            device_id={"cell": flip(my_cell, hop)},
            device_id_type=MESH,
        )

    def y_pass(chunk, rel):
        if rel:
            y_copy(chunk, rel, True).wait_recv()
        hop = (last_hop(rel) if rel else n_cell) // 2
        while hop:
            y_copy(chunk, rel | hop).start()
            hop //= 2

    def y_level(count):
        for chunk in range(Y_CHUNKS):
            for rel in sorted(range(n_cell), reverse=True):
                if bin(rel).count("1") == count:
                    y_pass(chunk, rel)

    y_level(0)
    for count in range(1, n_cell.bit_length()):
        y_level(count)
        if count <= levels:
            for chunk in range(X_CHUNKS):
                x_spread(chunk, levels - count)
    for count in range(n_cell.bit_length(), levels + 1):
        for chunk in range(X_CHUNKS):
            x_spread(chunk, levels - count)

    for chunk in range(X_CHUNKS):
        for level in range(levels):
            x_scatter(chunk, level).wait_send()
            x_gather(chunk, level).wait_send()
    for rel in range(1, n_cell):
        for chunk in range(Y_CHUNKS):
            y_copy(chunk, rel).wait_send()
        for p in range(PIECES):
            far_copy(p, rel).wait_send()
            swap_copy(p, rel, side).wait_send()
        for v in range(2 * ITERS):
            vec_copy(v, rel).wait_send()
    drain("desc", n_desc, my_desc, row_buf, row_send, row_recv, 2 * ITERS)
    drain("cell", n_cell, my_cell, col_buf, col_send, col_recv, 2 * ITERS - 1)


def run_plan(n_cell, n_desc, cells, descs, g_start, cot_f, cot_g):
    rows, width = cells.shape
    cols = descs.shape[0]
    vmem = pltpu.VMEM
    dma = pltpu.SemaphoreType.DMA
    spec = pl.BlockSpec(memory_space=pltpu.VMEM)
    n_row, n_col = 2 * ITERS, 2 * ITERS - 1
    x_levels = n_desc.bit_length() - 1
    n_kept = n_cell if n_cell <= 8 else 1
    return pl.pallas_call(
        functools.partial(plan_kernel, n_cell, n_desc),
        out_shape=(
            vmem((rows, width), F32),
            vmem((cols, width), F32),
        ),
        in_specs=[spec] * 5,
        out_specs=(spec, spec),
        scratch_shapes=[
            vmem((rows, cols), F32),
            vmem((rows, LANES), F32),
            vmem((rows, LANES), F32),
            vmem((rows, LANES), F32),
            vmem((8, cols), F32),
            vmem((8, cols), F32),
            vmem((8, cols), F32),
            vmem((rows, len(PAIRS) * width), BF16),
            vmem((cols, len(PAIRS) * width), BF16),
            vmem((2 * ITERS, rows), F32),
            vmem((2 * ITERS, cols), F32),
            vmem((1, cols), F32),
            vmem((rows, LANES), BF16),
            vmem((LANES, cols), BF16),
            vmem((n_row, n_desc, 1, rows), F32),
            vmem((n_col, n_cell, 1, cols), F32),
            dma((n_row, n_desc)),
            dma((n_row, n_desc)),
            dma((n_col, n_cell)),
            dma((n_col, n_cell)),
            vmem((rows, width), F32),
            vmem((rows, width), F32),
            dma((2, X_CHUNKS, x_levels)),
            dma((2, X_CHUNKS, x_levels)),
            vmem((n_cell, rows, width), F32),
            dma((PIECES, n_cell)),
            dma((PIECES, n_cell)),
            dma((PIECES, n_cell)),
            dma((PIECES, n_cell)),
            vmem((2 * ITERS, n_cell, 1, rows), F32),
            dma((2 * ITERS, n_cell)),
            dma((2 * ITERS, n_cell)),
            vmem((cols // n_cell, n_cell * rows), F32),
            vmem((cols // n_cell, LANES), F32),
            vmem((rows // 2, len(PAIRS) * width), BF16),
            vmem((n_kept * rows, width), BF16),
            vmem((n_kept * rows, width), BF16),
            vmem((cols // n_cell, width), F32),
            dma((Y_CHUNKS, n_cell)),
            dma((Y_CHUNKS, n_cell)),
        ],
        compiler_params=pltpu.CompilerParams(
            collective_id=0, has_side_effects=True, vmem_limit_bytes=60 * 1024 * 1024
        ),
        name="plan",
    )(cells, descs, g_start[None, :], cot_f[None, :], cot_g[None, :])


def solution(mesh):
    n_cell = mesh.shape["cell"]
    n_desc = mesh.shape["desc"]

    def on_device(cells, descs, g_start, cot_f, cot_g):
        return run_plan(n_cell, n_desc, cells, descs, g_start, cot_f, cot_g)

    placed = (P("cell", None), P("desc", None), P("desc"), P("cell"), P("desc"))
    return jax.shard_map(
        on_device,
        mesh=mesh,
        in_specs=placed,
        out_specs=(P("cell", None), P("desc", None)),
        check_vma=False,
    )
```

```python
import functools
import math

import jax
import jax.numpy as jnp
from jax import lax
from jax.experimental import pallas as pl
from jax.experimental.pallas import tpu as pltpu
from jax.sharding import PartitionSpec as P

ITERS = 4
MESH = pl.DeviceIdType.MESH
LANES = 128
F32 = jnp.float32
BF16 = jnp.bfloat16
LOG2E = math.log2(math.e)
X_CHUNKS = 2
Y_CHUNKS = 4
PIECES = 4
Y_PARTS = 2
FIRST_EXTRA = 2
PAIRS = ((0, 0), (0, 1), (1, 0), (0, 2), (2, 0), (1, 1))


def tree(op, parts):
    parts = list(parts)
    while len(parts) > 1:
        parts = [op(parts[i], parts[i + 1]) if i + 1 < len(parts) else parts[i] for i in range(0, len(parts), 2)]
    return parts[0]


def rotate(start, offset, count):
    return lax.rem(start + offset + count, count)


def split2(value):
    high = value.astype(BF16)
    return high, (value - high.astype(F32)).astype(BF16)


def split3(value):
    high = value.astype(BF16)
    rest = value - high.astype(F32)
    mid = rest.astype(BF16)
    return high, mid, (rest - mid.astype(F32)).astype(BF16)


def mm(a, b):
    return jnp.dot(a, b, preferred_element_type=F32)


def small_copy(axis, count, me, buf, send_sem, recv_sem, index, off):
    return pltpu.make_async_remote_copy(
        src_ref=buf.at[index, me],
        dst_ref=buf.at[index, me],
        send_sem=send_sem.at[index, off],
        recv_sem=recv_sem.at[index, me],
        device_id={axis: rotate(me, off, count)},
        device_id_type=MESH,
    )


def exchange(axis, count, me, buf, send_sem, recv_sem, index, between):
    for off in range(1, count):
        small_copy(axis, count, me, buf, send_sem, recv_sem, index, off).start()
    between()
    for off in range(1, count):
        source = rotate(me, -off, count)
        pltpu.make_async_remote_copy(
            src_ref=buf.at[index, source],
            dst_ref=buf.at[index, source],
            send_sem=send_sem.at[index, off],
            recv_sem=recv_sem.at[index, source],
            device_id={axis: rotate(me, off, count)},
            device_id_type=MESH,
        ).wait_recv()


def flip(index, bits):
    for bit in range(bits.bit_length()):
        if bits >> bit & 1:
            index = index + (1 - 2 * lax.rem(index // (1 << bit), 2)) * (1 << bit)
    return index


def last_hop(rel):
    return rel & -rel


def bulk_schedule(count, pieces, windows):
    top = count // 2
    limit = 2
    while True:
        came = {(p, 0): -1 for p in range(pieces)}
        plan = []
        for window in range(windows):
            left = {1 << b: limit + FIRST_EXTRA * (window == 0) for b in range(count.bit_length() - 1)}
            sent = []
            for hop in sorted(left, reverse=True):
                for (p, rel), when in sorted(came.items(), key=lambda item: (item[1], item[0])):
                    to = rel | hop
                    if when >= window or (p, to) in came or last_hop(to) != hop or rel & hop:
                        continue
                    cost = 2 if hop == top else 1
                    if left[hop] < cost:
                        continue
                    left[hop] -= cost
                    if hop == top and top > 1:
                        left[top // 2] -= 1
                    came[p, to] = window
                    sent.append((p, to))
            plan.append(sent)
        if len(came) == pieces * count:
            return plan
        limit += 1


def drain(axis, count, me, buf, send_sem, recv_sem, indices):
    for index in range(indices):
        for off in range(1, count):
            small_copy(axis, count, me, buf, send_sem, recv_sem, index, off).wait_send()


def combine(parts):
    top = tree(jnp.maximum, parts)
    return top + jnp.log(tree(jnp.add, [jnp.exp2(part - top) for part in parts])) * LOG2E


def plan_kernel(
    n_cell, n_desc,
    cells, descs, g_first, cf, cg,
    px, py,
    plan, vcol, racc_m, racc_s, cacc_m, cacc_s, wide,
    cat_c, cat_d, s_rows, t_rows, g_row, s_cat, t_cat,
    row_buf, col_buf, row_send, row_recv, col_send, col_recv,
    part_x, got_x, x_send, x_recv,
    far_cells, far_send, far_recv, swap_send, swap_recv,
    vec_buf, vec_send, vec_recv,
    slab, g_slab, cat_t, keep_h, keep_m, sum_y, y_send, y_recv,
):
    rows, width = cells.shape
    cols = descs.shape[0]
    scale = 2.0 / math.sqrt(width)
    my_cell = lax.axis_index("cell")
    my_desc = lax.axis_index("desc")
    side = lax.rem(my_desc, 2)
    blocks = cols // LANES
    y_block = cols // n_cell
    half = rows // 2
    piece = half // PIECES
    group = 16
    strips = 4
    keep = keep_h.shape[0] == n_cell * rows

    barrier = pltpu.get_barrier_semaphore()
    for off in range(1, n_desc):
        pl.semaphore_signal(barrier, inc=1, device_id={"desc": rotate(my_desc, off, n_desc)}, device_id_type=MESH)
    for off in range(1, n_cell):
        pl.semaphore_signal(barrier, inc=1, device_id={"cell": rotate(my_cell, off, n_cell)}, device_id_type=MESH)

    def lane(b):
        return slice(b * LANES, (b + 1) * LANES)

    def fill(cat, value, which):
        parts = split3(value)
        for n, pair in enumerate(PAIRS):
            cat[:, n * width:(n + 1) * width] = parts[pair[which]]
        return parts

    def contract(a, b):
        return lax.dot_general(a, b, (((1,), (1,)), ((), ())), preferred_element_type=F32)

    fill(cat_c, cells[...] * (scale * LOG2E), 0)
    fill(cat_d, descs[...], 1)

    pl.semaphore_wait(barrier, n_desc + n_cell - 2)

    schedule = bulk_schedule(n_cell, PIECES, 2 * ITERS - 1)

    def far_rows(p, which):
        return pl.ds(pl.multiple_of(which * half + p * piece, piece), piece)

    def far_copy(p, rel):
        hop = last_hop(rel)
        at = far_rows(p, side)
        return pltpu.make_async_remote_copy(
            src_ref=cells.at[at] if rel == hop else far_cells.at[rel ^ hop, at],
            dst_ref=far_cells.at[rel, at],
            send_sem=far_send.at[p, rel],
            recv_sem=far_recv.at[p, rel],
            device_id={"cell": flip(my_cell, hop)},
            device_id_type=MESH,
        )

    def swap_copy(p, rel, which):
        at = far_rows(p, which)
        return pltpu.make_async_remote_copy(
            src_ref=far_cells.at[rel, at],
            dst_ref=far_cells.at[rel, at],
            send_sem=swap_send.at[p, rel],
            recv_sem=swap_recv.at[p, rel],
            device_id={"desc": flip(my_desc, 1)},
            device_id_type=MESH,
        )

    def vec_copy(v, rel):
        return pltpu.make_async_remote_copy(
            src_ref=vec_buf.at[v, 0],
            dst_ref=vec_buf.at[v, rel],
            send_sem=vec_send.at[v, rel],
            recv_sem=vec_recv.at[v, rel],
            device_id={"cell": flip(my_cell, rel)},
            device_id_type=MESH,
        )

    def send_vec(v):
        for rel in range(1, n_cell):
            vec_copy(v, rel).start()

    my_slab = pl.ds(pl.multiple_of(my_cell * y_block, y_block), y_block)

    def slab_task(rel, which):
        start = pl.multiple_of(which * half, half)
        at = pl.ds(start, half)
        source = cells[at, :] if rel == 0 else far_cells[rel, at, :]
        parts = fill(cat_t, source * (scale * LOG2E), 0)
        if keep:
            put = pl.ds(pl.multiple_of(rel * rows + start, half), half)
            keep_h[put, :], keep_m[put, :] = parts[0], parts[1]
        logits = contract(cat_d[my_slab, :], cat_t[...])
        out = pl.ds(pl.multiple_of(rel * rows + start, half), half)
        g_here = jnp.concatenate([g_slab[...]] * (half // LANES), axis=1)
        slab[:, out] = jnp.exp2((logits + vec_buf[0, rel, :, at]) + g_here)

    tasks = [(0, side), (0, 1 - side)]
    seen = {}
    swapping = []
    ready = {0}

    def run_tasks(most):
        for _ in range(min(most, len(tasks))):
            rel, which = tasks.pop(0)
            if rel not in ready:
                vec_copy(0, rel).wait_recv()
                ready.add(rel)
            slab_task(rel, which)

    def window(w):
        arrived = schedule[w - 1] if 0 < w <= len(schedule) else []
        for p, rel in arrived:
            far_copy(p, rel).wait_recv()
        for p, rel in schedule[w] if w < len(schedule) else []:
            far_copy(p, rel).start()
        for p, rel in arrived:
            swap_copy(p, rel, side).start()
            swapping.append((p, rel))
            seen[rel] = seen.get(rel, 0) + 1
            if seen[rel] == PIECES:
                tasks.append((rel, side))

    def finish_swaps():
        for p, rel in swapping:
            swap_copy(p, rel, 1 - side).wait_recv()
            seen[rel, 1] = seen.get((rel, 1), 0) + 1
            if seen[rel, 1] == PIECES:
                tasks.append((rel, 1 - side))
        swapping.clear()

    window(0)

    def multiply(i, _):
        at = pl.ds(pl.multiple_of(i * 256, 256), 256)
        plan[at, :] = contract(cat_c[at, :], cat_d[...])
        return 0

    lax.fori_loop(0, rows // 256, multiply, 0)
    g_zero = g_first[...] * LOG2E
    wide[...] = jnp.broadcast_to(g_zero, (8, cols))

    def first_row(i, _):
        for u in range(strips):
            at = pl.ds(pl.multiple_of((i * strips + u) * 8, 8), 8)
            parts = [plan[at, lane(b)] + wide[:, lane(b)] for b in range(blocks)]
            top = tree(jnp.maximum, parts)
            racc_m[at, :] = top
            racc_s[at, :] = tree(jnp.add, [jnp.exp2(part - top) for part in parts])
        return 0

    lax.fori_loop(0, rows // (8 * strips), first_row, 0)
    tops = racc_m[...].T
    top = jnp.max(tops, axis=0, keepdims=True)
    total = jnp.sum(racc_s[...].T * jnp.exp2(tops - top), axis=0, keepdims=True)
    row_buf[0, my_desc] = top + jnp.log(total) * LOG2E
    exchange("desc", n_desc, my_desc, row_buf, row_send, row_recv, 0, lambda: None)
    f_one = -combine([row_buf[0, p] for p in range(n_desc)])
    vec_buf[0, 0] = f_one

    def spread_rows(vector):
        vcol[...] = jnp.broadcast_to(vector, (LANES, rows)).T

    spread_rows(f_one)
    cacc_m[...] = jnp.full((8, cols), -jnp.inf, F32)
    cacc_s[...] = jnp.zeros((8, cols), F32)

    def first_col(i, _):
        base = i * (8 * group)
        for b in range(blocks):
            ats = [pl.ds(pl.multiple_of(base + 8 * u, 8), 8) for u in range(group)]
            parts = [plan[at, lane(b)] + vcol[at, :] for at in ats]
            before = cacc_m[:, lane(b)]
            top = jnp.maximum(before, tree(jnp.maximum, parts))
            cacc_m[:, lane(b)] = top
            cacc_s[:, lane(b)] = cacc_s[:, lane(b)] * jnp.exp2(before - top) + tree(
                jnp.add, [jnp.exp2(part - top) for part in parts]
            )
        return 0

    lax.fori_loop(0, rows // (8 * group), first_col, 0)
    top = jnp.max(cacc_m[...], axis=0, keepdims=True)
    total = jnp.sum(cacc_s[...] * jnp.exp2(cacc_m[...] - top), axis=0, keepdims=True)
    col_buf[0, my_cell] = top + jnp.log(total) * LOG2E

    def after_first():
        send_vec(0)
        window(1)

    exchange("cell", n_cell, my_cell, col_buf, col_send, col_recv, 0, after_first)
    g_one = -combine([col_buf[0, p] for p in range(n_cell)])
    wide[...] = jnp.broadcast_to(g_one, (8, cols))
    g_row[...] = g_one
    g_slab[...] = jnp.broadcast_to(g_row[:, my_slab], (LANES, y_block)).T
    s_rows[0:1, :] = jnp.ones((1, rows), F32)
    t_rows[ITERS:ITERS + 1, :] = jnp.exp2(g_zero - g_one)
    t_rows[ITERS + 1:ITERS + 2, :] = jnp.ones((1, cols), F32)

    def make_plan(i, _):
        for u in range(strips):
            at = pl.ds(pl.multiple_of((i * strips + u) * 8, 8), 8)
            f_here = vcol[at, :]
            terms = []
            for b in range(blocks):
                value = jnp.exp2((plan[at, lane(b)] + f_here) + wide[:, lane(b)])
                plan[at, lane(b)] = value
                terms.append(value)
            racc_s[at, :] = tree(jnp.add, terms)
        return 0

    lax.fori_loop(0, rows // (8 * strips), make_plan, 0)

    def row_product(weight):
        wide[...] = jnp.broadcast_to(weight, (8, cols))
        weights = [wide[:, lane(b)] for b in range(blocks)]

        def body(i, _):
            for u in range(strips):
                at = pl.ds(pl.multiple_of((i * strips + u) * 8, 8), 8)
                racc_s[at, :] = tree(jnp.add, [plan[at, lane(b)] * weights[b] for b in range(blocks)])
            return 0

        lax.fori_loop(0, rows // (8 * strips), body, 0)

    def row_sum(index, most):
        def between():
            finish_swaps()
            run_tasks(most)

        row_buf[index, my_desc] = jnp.sum(racc_s[...].T, axis=0, keepdims=True)
        exchange("desc", n_desc, my_desc, row_buf, row_send, row_recv, index, between)
        return tree(jnp.add, [row_buf[index, p] for p in range(n_desc)])

    def col_sum(vector, v, index, w):
        def between():
            send_vec(v)
            window(w)
            run_tasks(3)

        def body(i, totals):
            for u in range(strips):
                at = pl.ds(pl.multiple_of((i * strips + u) * 8, 8), 8)
                here = vcol[at, :]
                totals = [totals[b] + plan[at, lane(b)] * here for b in range(blocks)]
            return totals

        vec_buf[v, 0] = vector
        spread_rows(vector)
        totals = lax.fori_loop(0, rows // (8 * strips), body, [jnp.zeros((8, LANES), F32)] * blocks)
        for b in range(blocks):
            col_buf[index, my_cell, :, lane(b)] = jnp.sum(totals[b], axis=0, keepdims=True)
        exchange("cell", n_cell, my_cell, col_buf, col_send, col_recv, index, between)
        return tree(jnp.add, [col_buf[index, p] for p in range(n_cell)])

    for k in range(1, ITERS):
        u_now = 1.0 / row_sum(k, 2)
        s_rows[k:k + 1, :] = u_now
        w_now = 1.0 / col_sum(u_now, k, k, k + 1)
        if k < ITERS - 1:
            t_rows[ITERS + 1 + k:ITERS + 2 + k, :] = w_now
            row_product(w_now)

    a_now = w_now * cg[...]
    for k in reversed(range(ITERS)):
        t = ITERS - 1 - k
        t_rows[k:k + 1, :] = a_now
        row_product(a_now)
        u_now = s_rows[k:k + 1, :]
        fbar = -(u_now * row_sum(ITERS + t, 2 if k > 0 else len(tasks) + 2 * n_cell))
        if k == ITERS - 1:
            fbar = fbar + cf[...]
        b_now = u_now * fbar
        s_rows[ITERS + k:ITERS + k + 1, :] = b_now
        if k > 0:
            w_before = t_rows[ITERS + k:ITERS + k + 1, :]
            a_now = -(w_before * (w_before * col_sum(b_now, ITERS + k, ITERS + t, ITERS + 1 + t)))
        else:
            vec_buf[ITERS, 0] = b_now
            send_vec(ITERS)

    pad = LANES - 2 * ITERS * len(PAIRS)

    def stack(value, which):
        parts = [part.astype(F32) for part in split3(value)]
        return jnp.concatenate([parts[pair[which]] for pair in PAIRS] + [jnp.zeros((pad, value.shape[1]), F32)], axis=0)

    s_cat[...] = stack(s_rows[...], 0).T.astype(BF16)
    t_cat[...] = stack(t_rows[...], 1).astype(BF16)

    x_chunk = rows // X_CHUNKS
    levels = n_desc.bit_length() - 1

    def x_plan(chunk):
        steps, start, size, place = [], chunk * x_chunk, x_chunk, chunk * x_chunk
        for bit in range(levels):
            mine = lax.rem(my_desc // (1 << bit), 2)
            size = size // 2
            sent = start + (1 - mine) * size
            start = start + mine * size
            steps.append((flip(my_desc, 1 << bit), pl.multiple_of(sent, 8), pl.multiple_of(start, 8), size, place))
            place += size
        return steps

    plans = [x_plan(chunk) for chunk in range(X_CHUNKS)]

    def x_scatter(chunk, level):
        peer, sent, kept, size, place = plans[chunk][level]
        return pltpu.make_async_remote_copy(
            src_ref=part_x.at[pl.ds(sent, size)],
            dst_ref=got_x.at[pl.ds(place, size)],
            send_sem=x_send.at[0, chunk, level],
            recv_sem=x_recv.at[0, chunk, level],
            device_id={"desc": peer},
            device_id_type=MESH,
        )

    def x_gather(chunk, level, arriving=False):
        peer, sent, kept, size, place = plans[chunk][level]
        at = pl.ds(sent if arriving else kept, size)
        return pltpu.make_async_remote_copy(
            src_ref=px.at[at],
            dst_ref=px.at[at],
            send_sem=x_send.at[1, chunk, level],
            recv_sem=x_recv.at[1, chunk, level],
            device_id={"desc": peer},
            device_id_type=MESH,
        )

    def x_add(chunk, level):
        peer, sent, kept, size, place = plans[chunk][level]
        x_scatter(chunk, level).wait_recv()
        out = part_x if level + 1 < levels else px
        out[pl.ds(kept, size), :] = part_x[pl.ds(kept, size), :] + got_x[pl.ds(place, size), :]
        if level + 1 < levels:
            x_scatter(chunk, level + 1).start()
        else:
            x_gather(chunk, level).start()

    def x_spread(chunk, level):
        x_gather(chunk, level, True).wait_recv()
        if level > 0:
            x_gather(chunk, level - 1).start()

    def x_tile(at):
        high, low = split2(plan[at, :] * mm(s_cat[at, :], t_cat[...]))
        d_high, d_low = cat_d[:, :width], cat_d[:, width:2 * width]
        part_x[at, :] = (-scale) * (mm(high, d_high) + (mm(low, d_high) + mm(high, d_low)))

    def x_chunk_tiles(chunk):
        for first in (True, False):
            peer, sent, kept, size, place = plans[chunk][0]
            x_tile(pl.ds(sent if first else kept, size))
            if first:
                x_scatter(chunk, 0).start()

    y_rows = y_block // Y_CHUNKS

    def y_copy(chunk, rel, arriving=False):
        hop = last_hop(rel)
        owner = flip(my_cell, rel if arriving else rel ^ hop)
        at = pl.ds(pl.multiple_of(owner * y_block + chunk * y_rows, y_rows), y_rows)
        return pltpu.make_async_remote_copy(
            src_ref=py.at[at],
            dst_ref=py.at[at],
            send_sem=y_send.at[chunk, rel],
            recv_sem=y_recv.at[chunk, rel],
            device_id={"cell": flip(my_cell, hop)},
            device_id_type=MESH,
        )

    def y_pass(chunk, rel):
        if rel:
            y_copy(chunk, rel, True).wait_recv()
        hop = (last_hop(rel) if rel else n_cell) // 2
        while hop:
            y_copy(chunk, rel | hop).start()
            hop //= 2

    def y_level(count, chunks):
        for chunk in chunks:
            for rel in sorted(range(n_cell), reverse=True):
                if bin(rel).count("1") == count:
                    y_pass(chunk, rel)

    x_chunk_tiles(0)

    for v in range(1, 2 * ITERS):
        for rel in range(1, n_cell):
            vec_copy(v, rel).wait_recv()
    t_part = stack(t_rows[:, my_slab], 1).T.astype(BF16)
    if not keep:
        far_cells[0] = cells[...]
    part = y_block // Y_PARTS
    part_chunks = Y_CHUNKS // Y_PARTS

    for h in range(Y_PARTS):
        rows_here = slice(h * part, (h + 1) * part)
        sum_y[rows_here, :] = jnp.zeros((part, width), F32)

        def y_step(rel, _):
            at = pl.ds(pl.multiple_of(rel * rows, rows), rows)
            s_here = jnp.concatenate(
                [jnp.ones((1, rows), F32)] + [vec_buf[v, rel] for v in range(1, 2 * ITERS)], axis=0
            )
            high, low = split2(slab[rows_here, at] * mm(t_part[rows_here], stack(s_here, 0).astype(BF16)))
            if keep:
                c_high, c_mid = keep_h[at, :], keep_m[at, :]
            else:
                c_high, c_mid = split2(far_cells[rel] * (scale * LOG2E))
            sum_y[rows_here, :] = sum_y[rows_here, :] + (mm(high, c_high) + (mm(low, c_high) + mm(high, c_mid)))
            return 0

        lax.fori_loop(0, n_cell, y_step, 0)
        py[pl.ds(pl.multiple_of(my_cell * y_block + h * part, part), part), :] = sum_y[rows_here, :] * (-1.0 / LOG2E)
        y_level(0, range(h * part_chunks, (h + 1) * part_chunks))
        if h == 0:
            for chunk in range(1):
                x_add(chunk, 0)
    for chunk in range(1, X_CHUNKS):
        x_chunk_tiles(chunk)

    y_level(1, range(part_chunks))
    for chunk in range(1, X_CHUNKS):
        x_add(chunk, 0)
    y_level(1, range(part_chunks, Y_CHUNKS))
    for level in range(1, levels):
        for chunk in range(X_CHUNKS):
            x_add(chunk, level)
    y_level(2, range(part_chunks))
    for chunk in range(X_CHUNKS):
        x_spread(chunk, levels - 1)
    y_level(2, range(part_chunks, Y_CHUNKS))
    for level in reversed(range(levels - 1)):
        for chunk in range(X_CHUNKS):
            x_spread(chunk, level)
    for count in range(3, n_cell.bit_length()):
        y_level(count, range(Y_CHUNKS))

    for chunk in range(X_CHUNKS):
        for level in range(levels):
            x_scatter(chunk, level).wait_send()
            x_gather(chunk, level).wait_send()
    for rel in range(1, n_cell):
        for chunk in range(Y_CHUNKS):
            y_copy(chunk, rel).wait_send()
        for p in range(PIECES):
            far_copy(p, rel).wait_send()
            swap_copy(p, rel, side).wait_send()
        for v in range(2 * ITERS):
            vec_copy(v, rel).wait_send()
    drain("desc", n_desc, my_desc, row_buf, row_send, row_recv, 2 * ITERS)
    drain("cell", n_cell, my_cell, col_buf, col_send, col_recv, 2 * ITERS - 1)


def run_plan(n_cell, n_desc, cells, descs, g_start, cot_f, cot_g):
    rows, width = cells.shape
    cols = descs.shape[0]
    vmem = pltpu.VMEM
    dma = pltpu.SemaphoreType.DMA
    spec = pl.BlockSpec(memory_space=pltpu.VMEM)
    n_row, n_col = 2 * ITERS, 2 * ITERS - 1
    x_levels = n_desc.bit_length() - 1
    n_kept = n_cell if n_cell <= 8 else 1
    return pl.pallas_call(
        functools.partial(plan_kernel, n_cell, n_desc),
        out_shape=(
            vmem((rows, width), F32),
            vmem((cols, width), F32),
        ),
        in_specs=[spec] * 5,
        out_specs=(spec, spec),
        scratch_shapes=[
            vmem((rows, cols), F32),
            vmem((rows, LANES), F32),
            vmem((rows, LANES), F32),
            vmem((rows, LANES), F32),
            vmem((8, cols), F32),
            vmem((8, cols), F32),
            vmem((8, cols), F32),
            vmem((rows, len(PAIRS) * width), BF16),
            vmem((cols, len(PAIRS) * width), BF16),
            vmem((2 * ITERS, rows), F32),
            vmem((2 * ITERS, cols), F32),
            vmem((1, cols), F32),
            vmem((rows, LANES), BF16),
            vmem((LANES, cols), BF16),
            vmem((n_row, n_desc, 1, rows), F32),
            vmem((n_col, n_cell, 1, cols), F32),
            dma((n_row, n_desc)),
            dma((n_row, n_desc)),
            dma((n_col, n_cell)),
            dma((n_col, n_cell)),
            vmem((rows, width), F32),
            vmem((rows, width), F32),
            dma((2, X_CHUNKS, x_levels)),
            dma((2, X_CHUNKS, x_levels)),
            vmem((n_cell, rows, width), F32),
            dma((PIECES, n_cell)),
            dma((PIECES, n_cell)),
            dma((PIECES, n_cell)),
            dma((PIECES, n_cell)),
            vmem((2 * ITERS, n_cell, 1, rows), F32),
            dma((2 * ITERS, n_cell)),
            dma((2 * ITERS, n_cell)),
            vmem((cols // n_cell, n_cell * rows), F32),
            vmem((cols // n_cell, LANES), F32),
            vmem((rows // 2, len(PAIRS) * width), BF16),
            vmem((n_kept * rows, width), BF16),
            vmem((n_kept * rows, width), BF16),
            vmem((cols // n_cell, width), F32),
            dma((Y_CHUNKS, n_cell)),
            dma((Y_CHUNKS, n_cell)),
        ],
        compiler_params=pltpu.CompilerParams(
            collective_id=0, has_side_effects=True, vmem_limit_bytes=60 * 1024 * 1024
        ),
        name="plan",
    )(cells, descs, g_start[None, :], cot_f[None, :], cot_g[None, :])


def solution(mesh):
    n_cell = mesh.shape["cell"]
    n_desc = mesh.shape["desc"]

    def on_device(cells, descs, g_start, cot_f, cot_g):
        return run_plan(n_cell, n_desc, cells, descs, g_start, cot_f, cot_g)

    placed = (P("cell", None), P("desc", None), P("desc"), P("cell"), P("desc"))
    return jax.shard_map(
        on_device,
        mesh=mesh,
        in_specs=placed,
        out_specs=(P("cell", None), P("desc", None)),
        check_vma=False,
    )
```

```python
import functools
import math

import jax
import jax.numpy as jnp
from jax import lax
from jax.experimental import pallas as pl
from jax.experimental.pallas import tpu as pltpu
from jax.sharding import PartitionSpec as P

ITERS = 4
MESH = pl.DeviceIdType.MESH
LANES = 128
F32 = jnp.float32
BF16 = jnp.bfloat16
LOG2E = math.log2(math.e)
Y_CHUNKS = 4
PIECES = 4
Y_PARTS = 2
FIRST_EXTRA = 2
PAIRS = ((0, 0), (0, 1), (1, 0), (0, 2), (2, 0), (1, 1))


def tree(op, parts):
    parts = list(parts)
    while len(parts) > 1:
        parts = [op(parts[i], parts[i + 1]) if i + 1 < len(parts) else parts[i] for i in range(0, len(parts), 2)]
    return parts[0]


def rotate(start, offset, count):
    return lax.rem(start + offset + count, count)


def split2(value):
    high = value.astype(BF16)
    return high, (value - high.astype(F32)).astype(BF16)


def split3(value):
    high = value.astype(BF16)
    rest = value - high.astype(F32)
    mid = rest.astype(BF16)
    return high, mid, (rest - mid.astype(F32)).astype(BF16)


def mm(a, b):
    return jnp.dot(a, b, preferred_element_type=F32)


def small_copy(axis, count, me, buf, send_sem, recv_sem, index, off):
    return pltpu.make_async_remote_copy(
        src_ref=buf.at[index, me],
        dst_ref=buf.at[index, me],
        send_sem=send_sem.at[index, off],
        recv_sem=recv_sem.at[index, me],
        device_id={axis: rotate(me, off, count)},
        device_id_type=MESH,
    )


def exchange(axis, count, me, buf, send_sem, recv_sem, index, between):
    for off in range(1, count):
        small_copy(axis, count, me, buf, send_sem, recv_sem, index, off).start()
    between()
    for off in range(1, count):
        source = rotate(me, -off, count)
        pltpu.make_async_remote_copy(
            src_ref=buf.at[index, source],
            dst_ref=buf.at[index, source],
            send_sem=send_sem.at[index, off],
            recv_sem=recv_sem.at[index, source],
            device_id={axis: rotate(me, off, count)},
            device_id_type=MESH,
        ).wait_recv()


def flip(index, bits):
    for bit in range(bits.bit_length()):
        if bits >> bit & 1:
            index = index + (1 - 2 * lax.rem(index // (1 << bit), 2)) * (1 << bit)
    return index


def last_hop(rel):
    return rel & -rel


def bulk_schedule(count, pieces, windows):
    top = count // 2
    limit = 2
    while True:
        came = {(p, 0): -1 for p in range(pieces)}
        plan = []
        for window in range(windows):
            left = {1 << b: limit + FIRST_EXTRA * (window == 0) for b in range(count.bit_length() - 1)}
            sent = []
            for hop in sorted(left, reverse=True):
                for (p, rel), when in sorted(came.items(), key=lambda item: (item[1], item[0])):
                    to = rel | hop
                    if when >= window or (p, to) in came or last_hop(to) != hop or rel & hop:
                        continue
                    cost = 2 if hop == top else 1
                    if left[hop] < cost:
                        continue
                    left[hop] -= cost
                    if hop == top and top > 1:
                        left[top // 2] -= 1
                    came[p, to] = window
                    sent.append((p, to))
            plan.append(sent)
        if len(came) == pieces * count:
            return plan
        limit += 1


def drain(axis, count, me, buf, send_sem, recv_sem, indices):
    for index in range(indices):
        for off in range(1, count):
            small_copy(axis, count, me, buf, send_sem, recv_sem, index, off).wait_send()


def combine(parts):
    top = tree(jnp.maximum, parts)
    return top + jnp.log(tree(jnp.add, [jnp.exp2(part - top) for part in parts])) * LOG2E


def plan_kernel(
    n_cell, n_desc,
    cells, descs, g_first, cf, cg,
    px, py,
    plan, vcol, racc_s, cacc_m, cacc_s, wide,
    cat_d, s_rows, t_rows, g_row, s_cat, t_cat, x_high, x_low,
    row_buf, col_buf, row_send, row_recv, col_send, col_recv,
    part_x, got_x, x_send, x_recv,
    far_cells, far_send, far_recv, swap_send, swap_recv,
    vec_buf, vec_send, vec_recv,
    slab, g_slab, cat_t, keep_h, keep_m, s_all, sum_y, y_send, y_recv,
):
    rows, width = cells.shape
    cols = descs.shape[0]
    scale = 2.0 / math.sqrt(width)
    my_cell = lax.axis_index("cell")
    my_desc = lax.axis_index("desc")
    side = lax.rem(my_desc, 2)
    blocks = cols // LANES
    y_block = cols // n_cell
    half = rows // 2
    piece = half // PIECES
    group = 16
    strips = 4
    keep = keep_h.shape[0] == n_cell * rows
    x_chunks = rows // (2 * x_high.shape[1])

    barrier = pltpu.get_barrier_semaphore()
    for off in range(1, n_desc):
        pl.semaphore_signal(barrier, inc=1, device_id={"desc": rotate(my_desc, off, n_desc)}, device_id_type=MESH)
    for off in range(1, n_cell):
        pl.semaphore_signal(barrier, inc=1, device_id={"cell": rotate(my_cell, off, n_cell)}, device_id_type=MESH)

    def lane(b):
        return slice(b * LANES, (b + 1) * LANES)

    def fill(cat, value, which):
        parts = split3(value)
        for n, pair in enumerate(PAIRS):
            cat[:, n * width:(n + 1) * width] = parts[pair[which]]
        return parts

    def contract(a, b):
        return lax.dot_general(a, b, (((1,), (1,)), ((), ())), preferred_element_type=F32)

    fill(cat_d, descs[...], 1)

    pl.semaphore_wait(barrier, n_desc + n_cell - 2)

    schedule = bulk_schedule(n_cell, PIECES, 2 * ITERS - 1)

    def far_rows(p, which):
        return pl.ds(pl.multiple_of(which * half + p * piece, piece), piece)

    def far_copy(p, rel):
        hop = last_hop(rel)
        at = far_rows(p, side)
        return pltpu.make_async_remote_copy(
            src_ref=cells.at[at] if rel == hop else far_cells.at[rel ^ hop, at],
            dst_ref=far_cells.at[rel, at],
            send_sem=far_send.at[p, rel],
            recv_sem=far_recv.at[p, rel],
            device_id={"cell": flip(my_cell, hop)},
            device_id_type=MESH,
        )

    def swap_copy(p, rel, which):
        at = far_rows(p, which)
        return pltpu.make_async_remote_copy(
            src_ref=far_cells.at[rel, at],
            dst_ref=far_cells.at[rel, at],
            send_sem=swap_send.at[p, rel],
            recv_sem=swap_recv.at[p, rel],
            device_id={"desc": flip(my_desc, 1)},
            device_id_type=MESH,
        )

    def vec_copy(v, rel):
        return pltpu.make_async_remote_copy(
            src_ref=vec_buf.at[v, 0],
            dst_ref=vec_buf.at[v, rel],
            send_sem=vec_send.at[v, rel],
            recv_sem=vec_recv.at[v, rel],
            device_id={"cell": flip(my_cell, rel)},
            device_id_type=MESH,
        )

    def send_vec(v):
        for rel in range(1, n_cell):
            vec_copy(v, rel).start()

    my_slab = pl.ds(pl.multiple_of(my_cell * y_block, y_block), y_block)

    def slab_task(rel, which):
        start = pl.multiple_of(which * half, half)
        at = pl.ds(start, half)
        source = cells[at, :] if rel == 0 else far_cells[rel, at, :]
        parts = fill(cat_t, source * (scale * LOG2E), 0)
        if keep:
            put = pl.ds(pl.multiple_of(rel * rows + start, half), half)
            keep_h[put, :], keep_m[put, :] = parts[0], parts[1]
        logits = contract(cat_d[my_slab, :], cat_t[...])
        out = pl.ds(pl.multiple_of(rel * rows + start, half), half)
        g_here = jnp.concatenate([g_slab[...]] * (half // LANES), axis=1)
        slab[:, out] = jnp.exp2((logits + vec_buf[0, rel, :, at]) + g_here)

    tasks = [(0, side), (0, 1 - side)]
    seen = {}
    swapping = []
    ready = {0}

    def run_tasks(most):
        for _ in range(min(most, len(tasks))):
            rel, which = tasks.pop(0)
            if rel not in ready:
                vec_copy(0, rel).wait_recv()
                ready.add(rel)
            slab_task(rel, which)

    def window(w):
        arrived = schedule[w - 1] if 0 < w <= len(schedule) else []
        for p, rel in arrived:
            far_copy(p, rel).wait_recv()
        for p, rel in schedule[w] if w < len(schedule) else []:
            far_copy(p, rel).start()
        for p, rel in arrived:
            swap_copy(p, rel, side).start()
            swapping.append((p, rel))
            seen[rel] = seen.get(rel, 0) + 1
            if seen[rel] == PIECES:
                tasks.append((rel, side))

    def finish_swaps():
        for p, rel in swapping:
            swap_copy(p, rel, 1 - side).wait_recv()
            seen[rel, 1] = seen.get((rel, 1), 0) + 1
            if seen[rel, 1] == PIECES:
                tasks.append((rel, 1 - side))
        swapping.clear()

    window(0)

    def multiply(i, _):
        at = pl.ds(pl.multiple_of(i * 256, 256), 256)
        use = cat_t.at[pl.ds(pl.multiple_of(lax.rem(i, half // 256) * 256, 256), 256)]
        fill(use, cells[at, :] * (scale * LOG2E), 0)
        plan[at, :] = contract(use[...], cat_d[...])
        return 0

    lax.fori_loop(0, rows // 256, multiply, 0)
    g_zero = g_first[...] * LOG2E
    wide[...] = jnp.broadcast_to(g_zero, (8, cols))

    def first_row(i, _):
        for u in range(strips):
            at = pl.ds(pl.multiple_of((i * strips + u) * 8, 8), 8)
            parts = [plan[at, lane(b)] + wide[:, lane(b)] for b in range(blocks)]
            top = tree(jnp.maximum, parts)
            vcol[at, :] = top
            racc_s[at, :] = tree(jnp.add, [jnp.exp2(part - top) for part in parts])
        return 0

    lax.fori_loop(0, rows // (8 * strips), first_row, 0)
    tops = vcol[...].T
    top = jnp.max(tops, axis=0, keepdims=True)
    total = jnp.sum(racc_s[...].T * jnp.exp2(tops - top), axis=0, keepdims=True)
    row_buf[0, my_desc] = top + jnp.log(total) * LOG2E
    exchange("desc", n_desc, my_desc, row_buf, row_send, row_recv, 0, lambda: None)
    f_one = -combine([row_buf[0, p] for p in range(n_desc)])
    vec_buf[0, 0] = f_one

    def spread_rows(vector):
        vcol[...] = jnp.broadcast_to(vector, (LANES, rows)).T

    spread_rows(f_one)
    cacc_m[...] = jnp.full((8, cols), -jnp.inf, F32)
    cacc_s[...] = jnp.zeros((8, cols), F32)

    def first_col(i, _):
        base = i * (8 * group)
        for b in range(blocks):
            ats = [pl.ds(pl.multiple_of(base + 8 * u, 8), 8) for u in range(group)]
            parts = [plan[at, lane(b)] + vcol[at, :] for at in ats]
            before = cacc_m[:, lane(b)]
            top = jnp.maximum(before, tree(jnp.maximum, parts))
            cacc_m[:, lane(b)] = top
            cacc_s[:, lane(b)] = cacc_s[:, lane(b)] * jnp.exp2(before - top) + tree(
                jnp.add, [jnp.exp2(part - top) for part in parts]
            )
        return 0

    lax.fori_loop(0, rows // (8 * group), first_col, 0)
    top = jnp.max(cacc_m[...], axis=0, keepdims=True)
    total = jnp.sum(cacc_s[...] * jnp.exp2(cacc_m[...] - top), axis=0, keepdims=True)
    col_buf[0, my_cell] = top + jnp.log(total) * LOG2E

    def after_first():
        send_vec(0)
        window(1)

    exchange("cell", n_cell, my_cell, col_buf, col_send, col_recv, 0, after_first)
    g_one = -combine([col_buf[0, p] for p in range(n_cell)])
    wide[...] = jnp.broadcast_to(g_one, (8, cols))
    g_row[...] = g_one
    g_slab[...] = jnp.broadcast_to(g_row[:, my_slab], (LANES, y_block)).T
    s_rows[0:1, :] = jnp.ones((1, rows), F32)
    t_rows[ITERS:ITERS + 1, :] = jnp.exp2(g_zero - g_one)
    t_rows[ITERS + 1:ITERS + 2, :] = jnp.ones((1, cols), F32)

    def make_plan(i, _):
        for u in range(strips):
            at = pl.ds(pl.multiple_of((i * strips + u) * 8, 8), 8)
            f_here = vcol[at, :]
            terms = []
            for b in range(blocks):
                value = jnp.exp2((plan[at, lane(b)] + f_here) + wide[:, lane(b)])
                plan[at, lane(b)] = value
                terms.append(value)
            racc_s[at, :] = tree(jnp.add, terms)
        return 0

    lax.fori_loop(0, rows // (8 * strips), make_plan, 0)

    def row_product(weight):
        wide[...] = jnp.broadcast_to(weight, (8, cols))
        weights = [wide[:, lane(b)] for b in range(blocks)]

        def body(i, _):
            for u in range(strips):
                at = pl.ds(pl.multiple_of((i * strips + u) * 8, 8), 8)
                racc_s[at, :] = tree(jnp.add, [plan[at, lane(b)] * weights[b] for b in range(blocks)])
            return 0

        lax.fori_loop(0, rows // (8 * strips), body, 0)

    def row_sum(index, most):
        def between():
            finish_swaps()
            run_tasks(most)

        row_buf[index, my_desc] = jnp.sum(racc_s[...].T, axis=0, keepdims=True)
        exchange("desc", n_desc, my_desc, row_buf, row_send, row_recv, index, between)
        return tree(jnp.add, [row_buf[index, p] for p in range(n_desc)])

    def col_sum(vector, v, index, w):
        def between():
            send_vec(v)
            window(w)
            run_tasks(3)

        def body(i, totals):
            for u in range(strips):
                at = pl.ds(pl.multiple_of((i * strips + u) * 8, 8), 8)
                here = vcol[at, :]
                totals = [totals[b] + plan[at, lane(b)] * here for b in range(blocks)]
            return totals

        vec_buf[v, 0] = vector
        spread_rows(vector)
        totals = lax.fori_loop(0, rows // (8 * strips), body, [jnp.zeros((8, LANES), F32)] * blocks)
        for b in range(blocks):
            col_buf[index, my_cell, :, lane(b)] = jnp.sum(totals[b], axis=0, keepdims=True)
        exchange("cell", n_cell, my_cell, col_buf, col_send, col_recv, index, between)
        return tree(jnp.add, [col_buf[index, p] for p in range(n_cell)])

    for k in range(1, ITERS):
        u_now = 1.0 / row_sum(k, 2)
        s_rows[k:k + 1, :] = u_now
        w_now = 1.0 / col_sum(u_now, k, k, k + 1)
        if k < ITERS - 1:
            t_rows[ITERS + 1 + k:ITERS + 2 + k, :] = w_now
            row_product(w_now)

    a_now = w_now * cg[...]
    for k in reversed(range(ITERS)):
        t = ITERS - 1 - k
        t_rows[k:k + 1, :] = a_now
        row_product(a_now)
        u_now = s_rows[k:k + 1, :]
        fbar = -(u_now * row_sum(ITERS + t, 2 if k > 0 else len(tasks) + 2 * n_cell))
        if k == ITERS - 1:
            fbar = fbar + cf[...]
        b_now = u_now * fbar
        s_rows[ITERS + k:ITERS + k + 1, :] = b_now
        if k > 0:
            w_before = t_rows[ITERS + k:ITERS + k + 1, :]
            a_now = -(w_before * (w_before * col_sum(b_now, ITERS + k, ITERS + t, ITERS + 1 + t)))
        else:
            vec_buf[ITERS, 0] = b_now
            send_vec(ITERS)

    pad = LANES - 2 * ITERS * len(PAIRS)

    def stack(value, which):
        parts = [part.astype(F32) for part in split3(value)]
        return jnp.concatenate([parts[pair[which]] for pair in PAIRS] + [jnp.zeros((pad, value.shape[1]), F32)], axis=0)

    s_cat[...] = stack(s_rows[...], 0).T.astype(BF16)
    t_cat[...] = stack(t_rows[...], 1).astype(BF16)

    x_chunk = rows // x_chunks
    levels = n_desc.bit_length() - 1

    def x_plan(chunk):
        steps, start, size, place = [], chunk * x_chunk, x_chunk, chunk * x_chunk
        for bit in range(levels):
            mine = lax.rem(my_desc // (1 << bit), 2)
            size = size // 2
            sent = start + (1 - mine) * size
            start = start + mine * size
            steps.append((flip(my_desc, 1 << bit), pl.multiple_of(sent, 8), pl.multiple_of(start, 8), size, place))
            place += size
        return steps

    plans = [x_plan(chunk) for chunk in range(x_chunks)]

    def x_scatter(chunk, level):
        peer, sent, kept, size, place = plans[chunk][level]
        return pltpu.make_async_remote_copy(
            src_ref=part_x.at[pl.ds(sent, size)],
            dst_ref=got_x.at[pl.ds(place, size)],
            send_sem=x_send.at[0, chunk, level],
            recv_sem=x_recv.at[0, chunk, level],
            device_id={"desc": peer},
            device_id_type=MESH,
        )

    def x_gather(chunk, level, arriving=False):
        peer, sent, kept, size, place = plans[chunk][level]
        at = pl.ds(sent if arriving else kept, size)
        return pltpu.make_async_remote_copy(
            src_ref=px.at[at],
            dst_ref=px.at[at],
            send_sem=x_send.at[1, chunk, level],
            recv_sem=x_recv.at[1, chunk, level],
            device_id={"desc": peer},
            device_id_type=MESH,
        )

    def x_add(chunk, level):
        peer, sent, kept, size, place = plans[chunk][level]
        x_scatter(chunk, level).wait_recv()
        out = part_x if level + 1 < levels else px
        out[pl.ds(kept, size), :] = part_x[pl.ds(kept, size), :] + got_x[pl.ds(place, size), :]
        if level + 1 < levels:
            x_scatter(chunk, level + 1).start()
        else:
            x_gather(chunk, level).start()

    def x_spread(chunk, level):
        x_gather(chunk, level, True).wait_recv()
        if level > 0:
            x_gather(chunk, level - 1).start()

    def x_make(at, slot):
        x_high[slot], x_low[slot] = split2(plan[at, :] * mm(s_cat[at, :], t_cat[...]))

    def x_use(at, slot):
        high, low = x_high[slot], x_low[slot]
        d_high, d_low = cat_d[:, :width], cat_d[:, width:2 * width]
        part_x[at, :] = (-scale) * (mm(high, d_high) + (mm(low, d_high) + mm(high, d_low)))

    def x_chunk_tiles(chunk):
        peer, sent, kept, size, place = plans[chunk][0]
        x_make(pl.ds(sent, size), 0)
        x_make(pl.ds(kept, size), 1)
        x_use(pl.ds(sent, size), 0)
        x_scatter(chunk, 0).start()
        x_use(pl.ds(kept, size), 1)

    down = [1 << bit for bit in reversed(range(n_cell.bit_length() - 1))]
    y_orders = [down[-1:] + down[:-1]] + [down] * (Y_CHUNKS - 1)
    y_starts = [y_block * eighth // 8 for eighth in (0, 1, 4, 6)]
    y_sizes = [y_block * eighth // 8 for eighth in (1, 3, 2, 2)]

    def y_after(chunk, rel):
        order = y_orders[chunk]
        return order[max([order.index(hop) + 1 for hop in order if rel & hop], default=0):]

    def y_copy(chunk, rel, arriving=False):
        hop = [hop for hop in y_orders[chunk] if rel & hop][-1]
        owner = flip(my_cell, rel if arriving else rel ^ hop)
        at = pl.ds(pl.multiple_of(owner * y_block + y_starts[chunk], 8), y_sizes[chunk])
        return pltpu.make_async_remote_copy(
            src_ref=py.at[at],
            dst_ref=py.at[at],
            send_sem=y_send.at[chunk, rel],
            recv_sem=y_recv.at[chunk, rel],
            device_id={"cell": flip(my_cell, hop)},
            device_id_type=MESH,
        )

    def y_pass(chunk, rel):
        if rel:
            y_copy(chunk, rel, True).wait_recv()
        for hop in y_after(chunk, rel):
            y_copy(chunk, rel | hop).start()

    def y_level(count, chunks):
        for chunk in chunks:
            for rel in sorted(range(n_cell), reverse=True):
                if bin(rel).count("1") == count:
                    y_pass(chunk, rel)

    x_chunk_tiles(0)

    for v in range(1, 2 * ITERS):
        for rel in range(1, n_cell):
            vec_copy(v, rel).wait_recv()
    t_part = stack(t_rows[:, my_slab], 1).T.astype(BF16)
    if not keep:
        far_cells[0] = cells[...]
    part = y_block // Y_PARTS
    part_chunks = Y_CHUNKS // Y_PARTS

    for rel in range(n_cell):
        s_here = jnp.concatenate(
            [jnp.ones((1, rows), F32)] + [vec_buf[v, rel] for v in range(1, 2 * ITERS)], axis=0
        )
        s_all[:, rel * rows:(rel + 1) * rows] = stack(s_here, 0).astype(BF16)

    for h in range(Y_PARTS):
        rows_here = slice(h * part, (h + 1) * part)
        sum_y[rows_here, :] = jnp.zeros((part, width), F32)

        def y_make(rel, slot):
            at = pl.ds(pl.multiple_of(rel * rows, rows), rows)
            high, low = split2(slab[rows_here, at] * mm(t_part[rows_here], s_all[:, at]))
            x_high[slot, rows_here, :rows], x_low[slot, rows_here, :rows] = high, low

        def y_use(rel, slot):
            at = pl.ds(pl.multiple_of(rel * rows, rows), rows)
            if keep:
                c_high, c_mid = keep_h[at, :], keep_m[at, :]
            else:
                c_high, c_mid = split2(far_cells[rel] * (scale * LOG2E))
            high, low = x_high[slot, rows_here, :rows], x_low[slot, rows_here, :rows]
            sum_y[rows_here, :] = sum_y[rows_here, :] + (mm(high, c_high) + (mm(low, c_high) + mm(high, c_mid)))

        def y_step(i, _):
            y_make(2 * i + 1, 1)
            y_use(2 * i, 0)
            y_make(jnp.minimum(2 * i + 2, n_cell - 1), 0)
            y_use(2 * i + 1, 1)
            return 0

        y_make(0, 0)
        lax.fori_loop(0, n_cell // 2, y_step, 0)
        py[pl.ds(pl.multiple_of(my_cell * y_block + h * part, part), part), :] = sum_y[rows_here, :] * (-1.0 / LOG2E)
        y_level(0, range(h * part_chunks, (h + 1) * part_chunks))
        if h == 0:
            for chunk in range(1):
                x_add(chunk, 0)
    for chunk in range(1, x_chunks):
        x_chunk_tiles(chunk)

    y_level(1, range(part_chunks))
    for chunk in range(1, x_chunks):
        x_add(chunk, 0)
    y_level(1, range(part_chunks, Y_CHUNKS))
    for level in range(1, levels):
        for chunk in range(x_chunks):
            x_add(chunk, level)
    y_level(2, range(part_chunks))
    for chunk in range(x_chunks):
        x_spread(chunk, levels - 1)
    y_level(2, range(part_chunks, Y_CHUNKS))
    for level in reversed(range(levels - 1)):
        for chunk in range(x_chunks):
            x_spread(chunk, level)
    for count in range(3, n_cell.bit_length()):
        y_level(count, range(Y_CHUNKS))

    for chunk in range(x_chunks):
        for level in range(levels):
            x_scatter(chunk, level).wait_send()
            x_gather(chunk, level).wait_send()
    for rel in range(1, n_cell):
        for chunk in range(Y_CHUNKS):
            y_copy(chunk, rel).wait_send()
        for p in range(PIECES):
            far_copy(p, rel).wait_send()
            swap_copy(p, rel, side).wait_send()
        for v in range(2 * ITERS):
            vec_copy(v, rel).wait_send()
    drain("desc", n_desc, my_desc, row_buf, row_send, row_recv, 2 * ITERS)
    drain("cell", n_cell, my_cell, col_buf, col_send, col_recv, 2 * ITERS - 1)


def run_plan(n_cell, n_desc, cells, descs, g_start, cot_f, cot_g):
    rows, width = cells.shape
    cols = descs.shape[0]
    vmem = pltpu.VMEM
    dma = pltpu.SemaphoreType.DMA
    spec = pl.BlockSpec(memory_space=pltpu.VMEM)
    n_row, n_col = 2 * ITERS, 2 * ITERS - 1
    x_levels = n_desc.bit_length() - 1
    kept, x_chunks = (n_cell * rows, 2) if n_cell <= 8 else (16, 4)
    return pl.pallas_call(
        functools.partial(plan_kernel, n_cell, n_desc),
        out_shape=(
            vmem((rows, width), F32),
            vmem((cols, width), F32),
        ),
        in_specs=[spec] * 5,
        out_specs=(spec, spec),
        scratch_shapes=[
            vmem((rows, cols), F32),
            vmem((rows, LANES), F32),
            vmem((rows, LANES), F32),
            vmem((8, cols), F32),
            vmem((8, cols), F32),
            vmem((8, cols), F32),
            vmem((cols, len(PAIRS) * width), BF16),
            vmem((2 * ITERS, rows), F32),
            vmem((2 * ITERS, cols), F32),
            vmem((1, cols), F32),
            vmem((rows, LANES), BF16),
            vmem((LANES, cols), BF16),
            vmem((2, rows // x_chunks // 2, cols), BF16),
            vmem((2, rows // x_chunks // 2, cols), BF16),
            vmem((n_row, n_desc, 1, rows), F32),
            vmem((n_col, n_cell, 1, cols), F32),
            dma((n_row, n_desc)),
            dma((n_row, n_desc)),
            dma((n_col, n_cell)),
            dma((n_col, n_cell)),
            vmem((rows, width), F32),
            vmem((rows, width), F32),
            dma((2, x_chunks, x_levels)),
            dma((2, x_chunks, x_levels)),
            vmem((n_cell, rows, width), F32),
            dma((PIECES, n_cell)),
            dma((PIECES, n_cell)),
            dma((PIECES, n_cell)),
            dma((PIECES, n_cell)),
            vmem((2 * ITERS, n_cell, 1, rows), F32),
            dma((2 * ITERS, n_cell)),
            dma((2 * ITERS, n_cell)),
            vmem((cols // n_cell, n_cell * rows), F32),
            vmem((cols // n_cell, LANES), F32),
            vmem((rows // 2, len(PAIRS) * width), BF16),
            vmem((kept, width), BF16),
            vmem((kept, width), BF16),
            vmem((LANES, n_cell * rows), BF16),
            vmem((cols // n_cell, width), F32),
            dma((Y_CHUNKS, n_cell)),
            dma((Y_CHUNKS, n_cell)),
        ],
        compiler_params=pltpu.CompilerParams(
            collective_id=0, has_side_effects=True, vmem_limit_bytes=60 * 1024 * 1024
        ),
        name="plan",
    )(cells, descs, g_start[None, :], cot_f[None, :], cot_g[None, :])


def solution(mesh):
    n_cell = mesh.shape["cell"]
    n_desc = mesh.shape["desc"]

    def on_device(cells, descs, g_start, cot_f, cot_g):
        return run_plan(n_cell, n_desc, cells, descs, g_start, cot_f, cot_g)

    placed = (P("cell", None), P("desc", None), P("desc"), P("cell"), P("desc"))
    return jax.shard_map(
        on_device,
        mesh=mesh,
        in_specs=placed,
        out_specs=(P("cell", None), P("desc", None)),
        check_vma=False,
    )
```

```python
import functools
import math

import jax
import jax.numpy as jnp
from jax import lax
from jax.experimental import pallas as pl
from jax.experimental.pallas import tpu as pltpu
from jax.sharding import PartitionSpec as P

ITERS = 4
MESH = pl.DeviceIdType.MESH
LANES = 128
F32 = jnp.float32
BF16 = jnp.bfloat16
LOG2E = math.log2(math.e)
Y_CHUNKS = 4
PIECES = 4
Y_PARTS = 2
FIRST_EXTRA = 0
PAIRS = ((0, 0), (0, 1), (1, 0), (0, 2), (2, 0), (1, 1))


def tree(op, parts):
    parts = list(parts)
    while len(parts) > 1:
        parts = [op(parts[i], parts[i + 1]) if i + 1 < len(parts) else parts[i] for i in range(0, len(parts), 2)]
    return parts[0]


def rotate(start, offset, count):
    return lax.rem(start + offset + count, count)


def split2(value):
    high = value.astype(BF16)
    return high, (value - high.astype(F32)).astype(BF16)


def split3(value):
    high = value.astype(BF16)
    rest = value - high.astype(F32)
    mid = rest.astype(BF16)
    return high, mid, (rest - mid.astype(F32)).astype(BF16)


def mm(a, b):
    return jnp.dot(a, b, preferred_element_type=F32)


def small_copy(axis, count, me, buf, send_sem, recv_sem, index, off):
    return pltpu.make_async_remote_copy(
        src_ref=buf.at[index, me],
        dst_ref=buf.at[index, me],
        send_sem=send_sem.at[index, off],
        recv_sem=recv_sem.at[index, me],
        device_id={axis: rotate(me, off, count)},
        device_id_type=MESH,
    )


def exchange(axis, count, me, buf, send_sem, recv_sem, index, between):
    for off in range(1, count):
        small_copy(axis, count, me, buf, send_sem, recv_sem, index, off).start()
    between()
    for off in range(1, count):
        source = rotate(me, -off, count)
        pltpu.make_async_remote_copy(
            src_ref=buf.at[index, source],
            dst_ref=buf.at[index, source],
            send_sem=send_sem.at[index, off],
            recv_sem=recv_sem.at[index, source],
            device_id={axis: rotate(me, off, count)},
            device_id_type=MESH,
        ).wait_recv()


def flip(index, bits):
    for bit in range(bits.bit_length()):
        if bits >> bit & 1:
            index = index + (1 - 2 * lax.rem(index // (1 << bit), 2)) * (1 << bit)
    return index


def last_hop(rel):
    return rel & -rel


def bulk_schedule(count, pieces, windows):
    top = count // 2
    limit = 3
    while True:
        came = {(p, 0): -1 for p in range(pieces)}
        plan = []
        for window in range(windows):
            left = {1 << b: limit + FIRST_EXTRA * (window == 0) for b in range(count.bit_length() - 1)}
            sent = []
            for hop in sorted(left, reverse=True):
                for (p, rel), when in sorted(came.items(), key=lambda item: (item[1], item[0])):
                    to = rel | hop
                    if when >= window or (p, to) in came or last_hop(to) != hop or rel & hop:
                        continue
                    cost = 2 if hop == top else 1
                    if left[hop] < cost:
                        continue
                    left[hop] -= cost
                    if hop == top and top > 1:
                        left[top // 2] -= 1
                    came[p, to] = window
                    sent.append((p, to))
            plan.append(sent)
        if len(came) == pieces * count:
            return plan
        limit += 1


def drain(axis, count, me, buf, send_sem, recv_sem, indices):
    for index in range(indices):
        for off in range(1, count):
            small_copy(axis, count, me, buf, send_sem, recv_sem, index, off).wait_send()


def combine(parts):
    top = tree(jnp.maximum, parts)
    return top + jnp.log(tree(jnp.add, [jnp.exp2(part - top) for part in parts])) * LOG2E


def plan_kernel(
    n_cell, n_desc,
    cells, descs, g_first, cf, cg,
    px, py,
    plan, vcol, racc_s, cacc_m, cacc_s, wide,
    cat_d, s_rows, t_rows, g_row, s_cat, t_cat, x_high, x_low,
    row_buf, col_buf, row_send, row_recv, col_send, col_recv,
    part_x, got_x, x_send, x_recv,
    far_cells, far_send, far_recv, swap_send, swap_recv,
    vec_buf, vec_send, vec_recv,
    slab, g_slab, cat_t, keep_h, keep_m, s_all, sum_y, y_send, y_recv,
):
    rows, width = cells.shape
    cols = descs.shape[0]
    scale = 2.0 / math.sqrt(width)
    my_cell = lax.axis_index("cell")
    my_desc = lax.axis_index("desc")
    side = lax.rem(my_desc, 2)
    blocks = cols // LANES
    y_block = cols // n_cell
    half = rows // 2
    piece = half // PIECES
    group = 16
    strips = 4
    keep = keep_h.shape[0] == n_cell * rows
    x_chunks = rows // (2 * x_high.shape[1])

    barrier = pltpu.get_barrier_semaphore()
    for off in range(1, n_desc):
        pl.semaphore_signal(barrier, inc=1, device_id={"desc": rotate(my_desc, off, n_desc)}, device_id_type=MESH)
    for off in range(1, n_cell):
        pl.semaphore_signal(barrier, inc=1, device_id={"cell": rotate(my_cell, off, n_cell)}, device_id_type=MESH)

    def lane(b):
        return slice(b * LANES, (b + 1) * LANES)

    def fill(cat, value, which):
        parts = split3(value)
        for n, pair in enumerate(PAIRS):
            cat[:, n * width:(n + 1) * width] = parts[pair[which]]
        return parts

    def contract(a, b):
        return lax.dot_general(a, b, (((1,), (1,)), ((), ())), preferred_element_type=F32)

    fill(cat_d, descs[...], 1)


    schedule = bulk_schedule(n_cell, PIECES, 2 * ITERS - 1)

    def far_rows(p, which):
        return pl.ds(pl.multiple_of(which * half + p * piece, piece), piece)

    def far_copy(p, rel):
        hop = last_hop(rel)
        at = far_rows(p, side)
        return pltpu.make_async_remote_copy(
            src_ref=cells.at[at] if rel == hop else far_cells.at[rel ^ hop, at],
            dst_ref=far_cells.at[rel, at],
            send_sem=far_send.at[p, rel],
            recv_sem=far_recv.at[p, rel],
            device_id={"cell": flip(my_cell, hop)},
            device_id_type=MESH,
        )

    def swap_copy(p, rel, which):
        at = far_rows(p, which)
        return pltpu.make_async_remote_copy(
            src_ref=far_cells.at[rel, at],
            dst_ref=far_cells.at[rel, at],
            send_sem=swap_send.at[p, rel],
            recv_sem=swap_recv.at[p, rel],
            device_id={"desc": flip(my_desc, 1)},
            device_id_type=MESH,
        )

    def vec_copy(v, rel):
        return pltpu.make_async_remote_copy(
            src_ref=vec_buf.at[v, 0],
            dst_ref=vec_buf.at[v, rel],
            send_sem=vec_send.at[v, rel],
            recv_sem=vec_recv.at[v, rel],
            device_id={"cell": flip(my_cell, rel)},
            device_id_type=MESH,
        )

    def send_vec(v):
        for rel in range(1, n_cell):
            vec_copy(v, rel).start()

    my_slab = pl.ds(pl.multiple_of(my_cell * y_block, y_block), y_block)

    def slab_task(rel, which):
        start = pl.multiple_of(which * half, half)
        at = pl.ds(start, half)
        source = cells[at, :] if rel == 0 else far_cells[rel, at, :]
        parts = fill(cat_t, source * (scale * LOG2E), 0)
        if keep:
            put = pl.ds(pl.multiple_of(rel * rows + start, half), half)
            keep_h[put, :], keep_m[put, :] = parts[0], parts[1]
        logits = contract(cat_d[my_slab, :], cat_t[...])
        out = pl.ds(pl.multiple_of(rel * rows + start, half), half)
        g_here = jnp.concatenate([g_slab[...]] * (half // LANES), axis=1)
        slab[:, out] = jnp.exp2((logits + vec_buf[0, rel, :, at]) + g_here)

    tasks = [(0, side), (0, 1 - side)]
    seen = {}
    swapping = []
    ready = {0}

    def run_tasks(most):
        for _ in range(min(most, len(tasks))):
            rel, which = tasks.pop(0)
            if rel not in ready:
                vec_copy(0, rel).wait_recv()
                ready.add(rel)
            slab_task(rel, which)

    def window(w):
        arrived = schedule[w - 1] if 0 < w <= len(schedule) else []
        for p, rel in arrived:
            far_copy(p, rel).wait_recv()
        for p, rel in schedule[w] if w < len(schedule) else []:
            far_copy(p, rel).start()
        for p, rel in arrived:
            swap_copy(p, rel, side).start()
            swapping.append((p, rel))
            seen[rel] = seen.get(rel, 0) + 1
            if seen[rel] == PIECES:
                tasks.append((rel, side))

    def finish_swaps():
        for p, rel in swapping:
            swap_copy(p, rel, 1 - side).wait_recv()
            seen[rel, 1] = seen.get((rel, 1), 0) + 1
            if seen[rel, 1] == PIECES:
                tasks.append((rel, 1 - side))
        swapping.clear()

    def multiply(i, _):
        at = pl.ds(pl.multiple_of(i * 256, 256), 256)
        use = cat_t.at[pl.ds(pl.multiple_of(lax.rem(i, half // 256) * 256, 256), 256)]
        fill(use, cells[at, :] * (scale * LOG2E), 0)
        plan[at, :] = contract(use[...], cat_d[...])
        return 0

    lax.fori_loop(0, rows // 256, multiply, 0)
    pl.semaphore_wait(barrier, n_desc + n_cell - 2)
    window(0)
    g_zero = g_first[...] * LOG2E
    wide[...] = jnp.broadcast_to(g_zero, (8, cols))

    def first_row(i, _):
        for u in range(strips):
            at = pl.ds(pl.multiple_of((i * strips + u) * 8, 8), 8)
            parts = [plan[at, lane(b)] + wide[:, lane(b)] for b in range(blocks)]
            top = tree(jnp.maximum, parts)
            vcol[at, :] = top
            racc_s[at, :] = tree(jnp.add, [jnp.exp2(part - top) for part in parts])
        return 0

    lax.fori_loop(0, rows // (8 * strips), first_row, 0)
    tops = vcol[...].T
    top = jnp.max(tops, axis=0, keepdims=True)
    total = jnp.sum(racc_s[...].T * jnp.exp2(tops - top), axis=0, keepdims=True)
    row_buf[0, my_desc] = top + jnp.log(total) * LOG2E
    exchange("desc", n_desc, my_desc, row_buf, row_send, row_recv, 0, lambda: None)
    f_one = -combine([row_buf[0, p] for p in range(n_desc)])
    vec_buf[0, 0] = f_one

    def spread_rows(vector):
        vcol[...] = jnp.broadcast_to(vector, (LANES, rows)).T

    spread_rows(f_one)
    cacc_m[...] = jnp.full((8, cols), -jnp.inf, F32)
    cacc_s[...] = jnp.zeros((8, cols), F32)

    def first_col(i, _):
        base = i * (8 * group)
        for b in range(blocks):
            ats = [pl.ds(pl.multiple_of(base + 8 * u, 8), 8) for u in range(group)]
            parts = [plan[at, lane(b)] + vcol[at, :] for at in ats]
            before = cacc_m[:, lane(b)]
            top = jnp.maximum(before, tree(jnp.maximum, parts))
            cacc_m[:, lane(b)] = top
            cacc_s[:, lane(b)] = cacc_s[:, lane(b)] * jnp.exp2(before - top) + tree(
                jnp.add, [jnp.exp2(part - top) for part in parts]
            )
        return 0

    lax.fori_loop(0, rows // (8 * group), first_col, 0)
    top = jnp.max(cacc_m[...], axis=0, keepdims=True)
    total = jnp.sum(cacc_s[...] * jnp.exp2(cacc_m[...] - top), axis=0, keepdims=True)
    col_buf[0, my_cell] = top + jnp.log(total) * LOG2E

    def after_first():
        send_vec(0)
        window(1)

    exchange("cell", n_cell, my_cell, col_buf, col_send, col_recv, 0, after_first)
    g_one = -combine([col_buf[0, p] for p in range(n_cell)])
    wide[...] = jnp.broadcast_to(g_one, (8, cols))
    g_row[...] = g_one
    g_slab[...] = jnp.broadcast_to(g_row[:, my_slab], (LANES, y_block)).T
    s_rows[0:1, :] = jnp.ones((1, rows), F32)
    t_rows[ITERS:ITERS + 1, :] = jnp.exp2(g_zero - g_one)
    t_rows[ITERS + 1:ITERS + 2, :] = jnp.ones((1, cols), F32)

    def make_plan(i, _):
        for u in range(strips):
            at = pl.ds(pl.multiple_of((i * strips + u) * 8, 8), 8)
            f_here = vcol[at, :]
            terms = []
            for b in range(blocks):
                value = jnp.exp2((plan[at, lane(b)] + f_here) + wide[:, lane(b)])
                plan[at, lane(b)] = value
                terms.append(value)
            racc_s[at, :] = tree(jnp.add, terms)
        return 0

    lax.fori_loop(0, rows // (8 * strips), make_plan, 0)

    def row_product(weight):
        wide[...] = jnp.broadcast_to(weight, (8, cols))
        weights = [wide[:, lane(b)] for b in range(blocks)]

        def body(i, _):
            for u in range(strips):
                at = pl.ds(pl.multiple_of((i * strips + u) * 8, 8), 8)
                racc_s[at, :] = tree(jnp.add, [plan[at, lane(b)] * weights[b] for b in range(blocks)])
            return 0

        lax.fori_loop(0, rows // (8 * strips), body, 0)

    def row_sum(index, most):
        def between():
            finish_swaps()
            run_tasks(most)

        row_buf[index, my_desc] = jnp.sum(racc_s[...].T, axis=0, keepdims=True)
        exchange("desc", n_desc, my_desc, row_buf, row_send, row_recv, index, between)
        return tree(jnp.add, [row_buf[index, p] for p in range(n_desc)])

    def col_sum(vector, v, index, w):
        def between():
            send_vec(v)
            window(w)
            run_tasks(3)

        def body(i, totals):
            for u in range(strips):
                at = pl.ds(pl.multiple_of((i * strips + u) * 8, 8), 8)
                here = vcol[at, :]
                totals = [totals[b] + plan[at, lane(b)] * here for b in range(blocks)]
            return totals

        vec_buf[v, 0] = vector
        spread_rows(vector)
        totals = lax.fori_loop(0, rows // (8 * strips), body, [jnp.zeros((8, LANES), F32)] * blocks)
        for b in range(blocks):
            col_buf[index, my_cell, :, lane(b)] = jnp.sum(totals[b], axis=0, keepdims=True)
        exchange("cell", n_cell, my_cell, col_buf, col_send, col_recv, index, between)
        return tree(jnp.add, [col_buf[index, p] for p in range(n_cell)])

    for k in range(1, ITERS):
        u_now = 1.0 / row_sum(k, 2)
        s_rows[k:k + 1, :] = u_now
        w_now = 1.0 / col_sum(u_now, k, k, k + 1)
        if k < ITERS - 1:
            t_rows[ITERS + 1 + k:ITERS + 2 + k, :] = w_now
            row_product(w_now)

    a_now = w_now * cg[...]
    for k in reversed(range(ITERS)):
        t = ITERS - 1 - k
        t_rows[k:k + 1, :] = a_now
        row_product(a_now)
        u_now = s_rows[k:k + 1, :]
        fbar = -(u_now * row_sum(ITERS + t, 2 if k > 0 else len(tasks) + 2 * n_cell))
        if k == ITERS - 1:
            fbar = fbar + cf[...]
        b_now = u_now * fbar
        s_rows[ITERS + k:ITERS + k + 1, :] = b_now
        if k > 0:
            w_before = t_rows[ITERS + k:ITERS + k + 1, :]
            a_now = -(w_before * (w_before * col_sum(b_now, ITERS + k, ITERS + t, ITERS + 1 + t)))
        else:
            vec_buf[ITERS, 0] = b_now
            send_vec(ITERS)

    pad = LANES - 2 * ITERS * len(PAIRS)

    def stack(value, which):
        parts = [part.astype(F32) for part in split3(value)]
        return jnp.concatenate([parts[pair[which]] for pair in PAIRS] + [jnp.zeros((pad, value.shape[1]), F32)], axis=0)

    s_cat[...] = stack(s_rows[...], 0).T.astype(BF16)
    t_cat[...] = stack(t_rows[...], 1).astype(BF16)

    x_chunk = rows // x_chunks
    levels = n_desc.bit_length() - 1

    def x_plan(chunk):
        steps, start, size, place = [], chunk * x_chunk, x_chunk, chunk * x_chunk
        for bit in range(levels):
            mine = lax.rem(my_desc // (1 << bit), 2)
            size = size // 2
            sent = start + (1 - mine) * size
            start = start + mine * size
            steps.append((flip(my_desc, 1 << bit), pl.multiple_of(sent, 8), pl.multiple_of(start, 8), size, place))
            place += size
        return steps

    plans = [x_plan(chunk) for chunk in range(x_chunks)]

    def x_scatter(chunk, level):
        peer, sent, kept, size, place = plans[chunk][level]
        return pltpu.make_async_remote_copy(
            src_ref=part_x.at[pl.ds(sent, size)],
            dst_ref=got_x.at[pl.ds(place, size)],
            send_sem=x_send.at[0, chunk, level],
            recv_sem=x_recv.at[0, chunk, level],
            device_id={"desc": peer},
            device_id_type=MESH,
        )

    def x_gather(chunk, level, arriving=False):
        peer, sent, kept, size, place = plans[chunk][level]
        at = pl.ds(sent if arriving else kept, size)
        return pltpu.make_async_remote_copy(
            src_ref=px.at[at],
            dst_ref=px.at[at],
            send_sem=x_send.at[1, chunk, level],
            recv_sem=x_recv.at[1, chunk, level],
            device_id={"desc": peer},
            device_id_type=MESH,
        )

    def x_add(chunk, level):
        peer, sent, kept, size, place = plans[chunk][level]
        x_scatter(chunk, level).wait_recv()
        out = part_x if level + 1 < levels else px
        out[pl.ds(kept, size), :] = part_x[pl.ds(kept, size), :] + got_x[pl.ds(place, size), :]
        if level + 1 < levels:
            x_scatter(chunk, level + 1).start()
        else:
            x_gather(chunk, level).start()

    def x_spread(chunk, level):
        x_gather(chunk, level, True).wait_recv()
        if level > 0:
            x_gather(chunk, level - 1).start()

    def x_make(at, slot):
        x_high[slot], x_low[slot] = split2(plan[at, :] * mm(s_cat[at, :], t_cat[...]))

    def x_use(at, slot):
        high, low = x_high[slot], x_low[slot]
        d_high, d_low = cat_d[:, :width], cat_d[:, width:2 * width]
        part_x[at, :] = (-scale) * (mm(high, d_high) + (mm(low, d_high) + mm(high, d_low)))

    def x_chunk_tiles(chunk):
        peer, sent, kept, size, place = plans[chunk][0]
        x_make(pl.ds(sent, size), 0)
        x_make(pl.ds(kept, size), 1)
        x_use(pl.ds(sent, size), 0)
        x_scatter(chunk, 0).start()
        x_use(pl.ds(kept, size), 1)

    down = [1 << bit for bit in reversed(range(n_cell.bit_length() - 1))]
    y_orders = [down[-1:] + down[:-1]] + [down] * (Y_CHUNKS - 1)
    y_starts = [y_block * eighth // 8 for eighth in (0, 1, 4, 6)]
    y_sizes = [y_block * eighth // 8 for eighth in (1, 3, 2, 2)]

    def y_after(chunk, rel):
        order = y_orders[chunk]
        return order[max([order.index(hop) + 1 for hop in order if rel & hop], default=0):]

    def y_copy(chunk, rel, arriving=False):
        hop = [hop for hop in y_orders[chunk] if rel & hop][-1]
        owner = flip(my_cell, rel if arriving else rel ^ hop)
        at = pl.ds(pl.multiple_of(owner * y_block + y_starts[chunk], 8), y_sizes[chunk])
        return pltpu.make_async_remote_copy(
            src_ref=py.at[at],
            dst_ref=py.at[at],
            send_sem=y_send.at[chunk, rel],
            recv_sem=y_recv.at[chunk, rel],
            device_id={"cell": flip(my_cell, hop)},
            device_id_type=MESH,
        )

    def y_pass(chunk, rel):
        if rel:
            y_copy(chunk, rel, True).wait_recv()
        for hop in y_after(chunk, rel):
            y_copy(chunk, rel | hop).start()

    def y_level(count, chunks):
        for chunk in chunks:
            for rel in sorted(range(n_cell), reverse=True):
                if bin(rel).count("1") == count:
                    y_pass(chunk, rel)

    x_chunk_tiles(0)

    for v in range(1, 2 * ITERS):
        for rel in range(1, n_cell):
            vec_copy(v, rel).wait_recv()
    t_part = stack(t_rows[:, my_slab], 1).T.astype(BF16)
    if not keep:
        far_cells[0] = cells[...]
    part = y_block // Y_PARTS
    part_chunks = Y_CHUNKS // Y_PARTS

    for rel in range(n_cell):
        s_here = jnp.concatenate(
            [jnp.ones((1, rows), F32)] + [vec_buf[v, rel] for v in range(1, 2 * ITERS)], axis=0
        )
        s_all[:, rel * rows:(rel + 1) * rows] = stack(s_here, 0).astype(BF16)

    for h in range(Y_PARTS):
        rows_here = slice(h * part, (h + 1) * part)
        sum_y[rows_here, :] = jnp.zeros((part, width), F32)

        def y_make(rel, slot):
            at = pl.ds(pl.multiple_of(rel * rows, rows), rows)
            high, low = split2(slab[rows_here, at] * mm(t_part[rows_here], s_all[:, at]))
            x_high[slot, rows_here, :rows], x_low[slot, rows_here, :rows] = high, low

        def y_use(rel, slot):
            at = pl.ds(pl.multiple_of(rel * rows, rows), rows)
            if keep:
                c_high, c_mid = keep_h[at, :], keep_m[at, :]
            else:
                c_high, c_mid = split2(far_cells[rel] * (scale * LOG2E))
            high, low = x_high[slot, rows_here, :rows], x_low[slot, rows_here, :rows]
            sum_y[rows_here, :] = sum_y[rows_here, :] + (mm(high, c_high) + (mm(low, c_high) + mm(high, c_mid)))

        def y_step(i, _):
            y_make(2 * i + 1, 1)
            y_use(2 * i, 0)
            y_make(jnp.minimum(2 * i + 2, n_cell - 1), 0)
            y_use(2 * i + 1, 1)
            return 0

        y_make(0, 0)
        lax.fori_loop(0, n_cell // 2, y_step, 0)
        py[pl.ds(pl.multiple_of(my_cell * y_block + h * part, part), part), :] = sum_y[rows_here, :] * (-1.0 / LOG2E)
        y_level(0, range(h * part_chunks, (h + 1) * part_chunks))
        if h == 0:
            for chunk in range(1):
                x_add(chunk, 0)
    for chunk in range(1, x_chunks):
        x_chunk_tiles(chunk)

    y_level(1, range(part_chunks))
    for chunk in range(1, x_chunks):
        x_add(chunk, 0)
    y_level(1, range(part_chunks, Y_CHUNKS))
    for level in range(1, levels):
        for chunk in range(x_chunks):
            x_add(chunk, level)
    y_level(2, range(part_chunks))
    for chunk in range(x_chunks):
        x_spread(chunk, levels - 1)
    y_level(2, range(part_chunks, Y_CHUNKS))
    for level in reversed(range(levels - 1)):
        for chunk in range(x_chunks):
            x_spread(chunk, level)
    for count in range(3, n_cell.bit_length()):
        y_level(count, range(Y_CHUNKS))

    for chunk in range(x_chunks):
        for level in range(levels):
            x_scatter(chunk, level).wait_send()
            x_gather(chunk, level).wait_send()
    for rel in range(1, n_cell):
        for chunk in range(Y_CHUNKS):
            y_copy(chunk, rel).wait_send()
        for p in range(PIECES):
            far_copy(p, rel).wait_send()
            swap_copy(p, rel, side).wait_send()
        for v in range(2 * ITERS):
            vec_copy(v, rel).wait_send()
    drain("desc", n_desc, my_desc, row_buf, row_send, row_recv, 2 * ITERS)
    drain("cell", n_cell, my_cell, col_buf, col_send, col_recv, 2 * ITERS - 1)


def run_plan(n_cell, n_desc, cells, descs, g_start, cot_f, cot_g):
    rows, width = cells.shape
    cols = descs.shape[0]
    vmem = pltpu.VMEM
    dma = pltpu.SemaphoreType.DMA
    spec = pl.BlockSpec(memory_space=pltpu.VMEM)
    n_row, n_col = 2 * ITERS, 2 * ITERS - 1
    x_levels = n_desc.bit_length() - 1
    kept, x_chunks = (n_cell * rows, 2) if n_cell <= 8 else (16, 4)
    return pl.pallas_call(
        functools.partial(plan_kernel, n_cell, n_desc),
        out_shape=(
            vmem((rows, width), F32),
            vmem((cols, width), F32),
        ),
        in_specs=[spec] * 5,
        out_specs=(spec, spec),
        scratch_shapes=[
            vmem((rows, cols), F32),
            vmem((rows, LANES), F32),
            vmem((rows, LANES), F32),
            vmem((8, cols), F32),
            vmem((8, cols), F32),
            vmem((8, cols), F32),
            vmem((cols, len(PAIRS) * width), BF16),
            vmem((2 * ITERS, rows), F32),
            vmem((2 * ITERS, cols), F32),
            vmem((1, cols), F32),
            vmem((rows, LANES), BF16),
            vmem((LANES, cols), BF16),
            vmem((2, rows // x_chunks // 2, cols), BF16),
            vmem((2, rows // x_chunks // 2, cols), BF16),
            vmem((n_row, n_desc, 1, rows), F32),
            vmem((n_col, n_cell, 1, cols), F32),
            dma((n_row, n_desc)),
            dma((n_row, n_desc)),
            dma((n_col, n_cell)),
            dma((n_col, n_cell)),
            vmem((rows, width), F32),
            vmem((rows, width), F32),
            dma((2, x_chunks, x_levels)),
            dma((2, x_chunks, x_levels)),
            vmem((n_cell, rows, width), F32),
            dma((PIECES, n_cell)),
            dma((PIECES, n_cell)),
            dma((PIECES, n_cell)),
            dma((PIECES, n_cell)),
            vmem((2 * ITERS, n_cell, 1, rows), F32),
            dma((2 * ITERS, n_cell)),
            dma((2 * ITERS, n_cell)),
            vmem((cols // n_cell, n_cell * rows), F32),
            vmem((cols // n_cell, LANES), F32),
            vmem((rows // 2, len(PAIRS) * width), BF16),
            vmem((kept, width), BF16),
            vmem((kept, width), BF16),
            vmem((LANES, n_cell * rows), BF16),
            vmem((cols // n_cell, width), F32),
            dma((Y_CHUNKS, n_cell)),
            dma((Y_CHUNKS, n_cell)),
        ],
        compiler_params=pltpu.CompilerParams(
            collective_id=0, has_side_effects=True, vmem_limit_bytes=60 * 1024 * 1024
        ),
        name="plan",
    )(cells, descs, g_start[None, :], cot_f[None, :], cot_g[None, :])


def solution(mesh):
    n_cell = mesh.shape["cell"]
    n_desc = mesh.shape["desc"]

    def on_device(cells, descs, g_start, cot_f, cot_g):
        return run_plan(n_cell, n_desc, cells, descs, g_start, cot_f, cot_g)

    placed = (P("cell", None), P("desc", None), P("desc"), P("cell"), P("desc"))
    return jax.shard_map(
        on_device,
        mesh=mesh,
        in_specs=placed,
        out_specs=(P("cell", None), P("desc", None)),
        check_vma=False,
    )
```

```python
import functools
import math

import jax
import jax.numpy as jnp
from jax import lax
from jax.experimental import pallas as pl
from jax.experimental.pallas import tpu as pltpu
from jax.sharding import PartitionSpec as P

ITERS = 4
MESH = pl.DeviceIdType.MESH
LANES = 128
F32 = jnp.float32
BF16 = jnp.bfloat16
LOG2E = math.log2(math.e)
Y_CHUNKS = 4
PIECES = 4
Y_PARTS = 2
FIRST_EXTRA = 0
PAIRS = ((0, 0), (0, 1), (1, 0), (0, 2), (2, 0), (1, 1))


def tree(op, parts):
    parts = list(parts)
    while len(parts) > 1:
        parts = [op(parts[i], parts[i + 1]) if i + 1 < len(parts) else parts[i] for i in range(0, len(parts), 2)]
    return parts[0]


def rotate(start, offset, count):
    return lax.rem(start + offset + count, count)


def split2(value):
    high = value.astype(BF16)
    return high, (value - high.astype(F32)).astype(BF16)


def split3(value):
    high = value.astype(BF16)
    rest = value - high.astype(F32)
    mid = rest.astype(BF16)
    return high, mid, (rest - mid.astype(F32)).astype(BF16)


def mm(a, b):
    return jnp.dot(a, b, preferred_element_type=F32)


def small_copy(axis, count, me, buf, send_sem, recv_sem, index, off):
    return pltpu.make_async_remote_copy(
        src_ref=buf.at[index, me],
        dst_ref=buf.at[index, me],
        send_sem=send_sem.at[index, off],
        recv_sem=recv_sem.at[index, me],
        device_id={axis: rotate(me, off, count)},
        device_id_type=MESH,
    )


def exchange(axis, count, me, buf, send_sem, recv_sem, index, between):
    for off in sorted(range(1, count), key=lambda steps: min(steps, count - steps)):
        small_copy(axis, count, me, buf, send_sem, recv_sem, index, off).start()
    between()
    for off in range(1, count):
        source = rotate(me, -off, count)
        pltpu.make_async_remote_copy(
            src_ref=buf.at[index, source],
            dst_ref=buf.at[index, source],
            send_sem=send_sem.at[index, off],
            recv_sem=recv_sem.at[index, source],
            device_id={axis: rotate(me, off, count)},
            device_id_type=MESH,
        ).wait_recv()


def flip(index, bits):
    for bit in range(bits.bit_length()):
        if bits >> bit & 1:
            index = index + (1 - 2 * lax.rem(index // (1 << bit), 2)) * (1 << bit)
    return index


def last_hop(rel):
    return rel & -rel


def bulk_schedule(count, pieces, windows):
    top = count // 2
    limit = 3
    while True:
        came = {(p, 0): -1 for p in range(pieces)}
        plan = []
        for window in range(windows):
            left = {1 << b: limit + FIRST_EXTRA * (window == 0) for b in range(count.bit_length() - 1)}
            sent = []
            for hop in sorted(left, reverse=True):
                for (p, rel), when in sorted(came.items(), key=lambda item: (item[1], item[0])):
                    to = rel | hop
                    if when >= window or (p, to) in came or last_hop(to) != hop or rel & hop:
                        continue
                    cost = 2 if hop == top else 1
                    if left[hop] < cost:
                        continue
                    left[hop] -= cost
                    if hop == top and top > 1:
                        left[top // 2] -= 1
                    came[p, to] = window
                    sent.append((p, to))
            plan.append(sent)
        if len(came) == pieces * count:
            return plan
        limit += 1


def drain(axis, count, me, buf, send_sem, recv_sem, indices):
    for index in range(indices):
        for off in range(1, count):
            small_copy(axis, count, me, buf, send_sem, recv_sem, index, off).wait_send()


def combine(parts):
    top = tree(jnp.maximum, parts)
    return top + jnp.log(tree(jnp.add, [jnp.exp2(part - top) for part in parts])) * LOG2E


def plan_kernel(
    n_cell, n_desc,
    cells, descs, g_first, cf, cg,
    px, py,
    plan, vcol, racc_s, cacc_m, cacc_s, wide,
    cat_d, s_rows, t_rows, g_row, s_cat, t_cat, x_high, x_low,
    row_buf, col_buf, row_send, row_recv, col_send, col_recv,
    part_x, got_x, x_send, x_recv,
    far_cells, far_send, far_recv, swap_send, swap_recv,
    vec_buf, vec_send, vec_recv,
    slab, g_slab, cat_t, keep_h, keep_m, s_all, sum_y, y_send, y_recv,
):
    rows, width = cells.shape
    cols = descs.shape[0]
    scale = 2.0 / math.sqrt(width)
    my_cell = lax.axis_index("cell")
    my_desc = lax.axis_index("desc")
    side = lax.rem(my_desc, 2)
    blocks = cols // LANES
    y_block = cols // n_cell
    half = rows // 2
    piece = half // PIECES
    group = 16
    strips = 4
    keep = keep_h.shape[0] == n_cell * rows
    x_chunks = rows // (2 * x_high.shape[1])

    barrier = pltpu.get_barrier_semaphore()
    for off in range(1, n_desc):
        pl.semaphore_signal(barrier, inc=1, device_id={"desc": rotate(my_desc, off, n_desc)}, device_id_type=MESH)
    for off in range(1, n_cell):
        pl.semaphore_signal(barrier, inc=1, device_id={"cell": rotate(my_cell, off, n_cell)}, device_id_type=MESH)

    def lane(b):
        return slice(b * LANES, (b + 1) * LANES)

    def fill(cat, value, which):
        parts = split3(value)
        for n, pair in enumerate(PAIRS):
            cat[:, n * width:(n + 1) * width] = parts[pair[which]]
        return parts

    def contract(a, b):
        return lax.dot_general(a, b, (((1,), (1,)), ((), ())), preferred_element_type=F32)

    fill(cat_d, descs[...], 1)


    schedule = bulk_schedule(n_cell, PIECES, 2 * ITERS - 1)

    def far_rows(p, which):
        return pl.ds(pl.multiple_of(which * half + p * piece, piece), piece)

    def far_copy(p, rel):
        hop = last_hop(rel)
        at = far_rows(p, side)
        return pltpu.make_async_remote_copy(
            src_ref=cells.at[at] if rel == hop else far_cells.at[rel ^ hop, at],
            dst_ref=far_cells.at[rel, at],
            send_sem=far_send.at[p, rel],
            recv_sem=far_recv.at[p, rel],
            device_id={"cell": flip(my_cell, hop)},
            device_id_type=MESH,
        )

    def swap_copy(p, rel, which):
        at = far_rows(p, which)
        return pltpu.make_async_remote_copy(
            src_ref=far_cells.at[rel, at],
            dst_ref=far_cells.at[rel, at],
            send_sem=swap_send.at[p, rel],
            recv_sem=swap_recv.at[p, rel],
            device_id={"desc": flip(my_desc, 1)},
            device_id_type=MESH,
        )

    def vec_copy(v, rel):
        return pltpu.make_async_remote_copy(
            src_ref=vec_buf.at[v, 0],
            dst_ref=vec_buf.at[v, rel],
            send_sem=vec_send.at[v, rel],
            recv_sem=vec_recv.at[v, rel],
            device_id={"cell": flip(my_cell, rel)},
            device_id_type=MESH,
        )

    def send_vec(v):
        for rel in reversed(range(1, n_cell)):
            vec_copy(v, rel).start()

    my_slab = pl.ds(pl.multiple_of(my_cell * y_block, y_block), y_block)

    def slab_task(rel, which):
        start = pl.multiple_of(which * half, half)
        at = pl.ds(start, half)
        source = cells[at, :] if rel == 0 else far_cells[rel, at, :]
        parts = fill(cat_t, source * (scale * LOG2E), 0)
        if keep:
            put = pl.ds(pl.multiple_of(rel * rows + start, half), half)
            keep_h[put, :], keep_m[put, :] = parts[0], parts[1]
        logits = contract(cat_d[my_slab, :], cat_t[...])
        out = pl.ds(pl.multiple_of(rel * rows + start, half), half)
        g_here = jnp.concatenate([g_slab[...]] * (half // LANES), axis=1)
        slab[:, out] = jnp.exp2((logits + vec_buf[0, rel, :, at]) + g_here)

    tasks = [(0, side), (0, 1 - side)]
    seen = {}
    swapping = []
    ready = {0}

    def run_tasks(most):
        for _ in range(min(most, len(tasks))):
            rel, which = tasks.pop(0)
            if rel not in ready:
                vec_copy(0, rel).wait_recv()
                ready.add(rel)
            slab_task(rel, which)

    def window(w):
        arrived = schedule[w - 1] if 0 < w <= len(schedule) else []
        for p, rel in arrived:
            far_copy(p, rel).wait_recv()
        for p, rel in schedule[w] if w < len(schedule) else []:
            far_copy(p, rel).start()
        for p, rel in arrived:
            swap_copy(p, rel, side).start()
            swapping.append((p, rel))
            seen[rel] = seen.get(rel, 0) + 1
            if seen[rel] == PIECES:
                tasks.append((rel, side))

    def finish_swaps():
        for p, rel in swapping:
            swap_copy(p, rel, 1 - side).wait_recv()
            seen[rel, 1] = seen.get((rel, 1), 0) + 1
            if seen[rel, 1] == PIECES:
                tasks.append((rel, 1 - side))
        swapping.clear()

    def multiply(i, _):
        at = pl.ds(pl.multiple_of(i * 256, 256), 256)
        use = cat_t.at[pl.ds(pl.multiple_of(lax.rem(i, half // 256) * 256, 256), 256)]
        fill(use, cells[at, :] * (scale * LOG2E), 0)
        plan[at, :] = contract(use[...], cat_d[...])
        return 0

    lax.fori_loop(0, rows // 256, multiply, 0)
    pl.semaphore_wait(barrier, n_desc + n_cell - 2)
    window(0)
    g_zero = g_first[...] * LOG2E
    wide[...] = jnp.broadcast_to(g_zero, (8, cols))

    def first_row(i, _):
        for u in range(strips):
            at = pl.ds(pl.multiple_of((i * strips + u) * 8, 8), 8)
            parts = [plan[at, lane(b)] + wide[:, lane(b)] for b in range(blocks)]
            top = tree(jnp.maximum, parts)
            vcol[at, :] = top
            racc_s[at, :] = tree(jnp.add, [jnp.exp2(part - top) for part in parts])
        return 0

    lax.fori_loop(0, rows // (8 * strips), first_row, 0)
    tops = vcol[...].T
    top = jnp.max(tops, axis=0, keepdims=True)
    total = jnp.sum(racc_s[...].T * jnp.exp2(tops - top), axis=0, keepdims=True)
    row_buf[0, my_desc] = top + jnp.log(total) * LOG2E
    exchange("desc", n_desc, my_desc, row_buf, row_send, row_recv, 0, lambda: None)
    f_one = -combine([row_buf[0, p] for p in range(n_desc)])
    vec_buf[0, 0] = f_one

    def spread_rows(vector):
        vcol[...] = jnp.broadcast_to(vector, (LANES, rows)).T

    spread_rows(f_one)
    cacc_m[...] = jnp.full((8, cols), -jnp.inf, F32)
    cacc_s[...] = jnp.zeros((8, cols), F32)

    def first_col(i, _):
        base = i * (8 * group)
        for b in range(blocks):
            ats = [pl.ds(pl.multiple_of(base + 8 * u, 8), 8) for u in range(group)]
            parts = [plan[at, lane(b)] + vcol[at, :] for at in ats]
            before = cacc_m[:, lane(b)]
            top = jnp.maximum(before, tree(jnp.maximum, parts))
            cacc_m[:, lane(b)] = top
            cacc_s[:, lane(b)] = cacc_s[:, lane(b)] * jnp.exp2(before - top) + tree(
                jnp.add, [jnp.exp2(part - top) for part in parts]
            )
        return 0

    lax.fori_loop(0, rows // (8 * group), first_col, 0)
    top = jnp.max(cacc_m[...], axis=0, keepdims=True)
    total = jnp.sum(cacc_s[...] * jnp.exp2(cacc_m[...] - top), axis=0, keepdims=True)
    col_buf[0, my_cell] = top + jnp.log(total) * LOG2E

    def after_first():
        send_vec(0)
        window(1)

    exchange("cell", n_cell, my_cell, col_buf, col_send, col_recv, 0, after_first)
    g_one = -combine([col_buf[0, p] for p in range(n_cell)])
    wide[...] = jnp.broadcast_to(g_one, (8, cols))
    g_row[...] = g_one
    g_slab[...] = jnp.broadcast_to(g_row[:, my_slab], (LANES, y_block)).T
    s_rows[0:1, :] = jnp.ones((1, rows), F32)
    t_rows[ITERS:ITERS + 1, :] = jnp.exp2(g_zero - g_one)
    t_rows[ITERS + 1:ITERS + 2, :] = jnp.ones((1, cols), F32)

    def make_plan(i, _):
        for u in range(strips):
            at = pl.ds(pl.multiple_of((i * strips + u) * 8, 8), 8)
            f_here = vcol[at, :]
            terms = []
            for b in range(blocks):
                value = jnp.exp2((plan[at, lane(b)] + f_here) + wide[:, lane(b)])
                plan[at, lane(b)] = value
                terms.append(value)
            racc_s[at, :] = tree(jnp.add, terms)
        return 0

    lax.fori_loop(0, rows // (8 * strips), make_plan, 0)

    def row_product(weight):
        wide[...] = jnp.broadcast_to(weight, (8, cols))
        weights = [wide[:, lane(b)] for b in range(blocks)]

        def body(i, _):
            for u in range(strips):
                at = pl.ds(pl.multiple_of((i * strips + u) * 8, 8), 8)
                racc_s[at, :] = tree(jnp.add, [plan[at, lane(b)] * weights[b] for b in range(blocks)])
            return 0

        lax.fori_loop(0, rows // (8 * strips), body, 0)

    def row_sum(index, most):
        def between():
            finish_swaps()
            run_tasks(most)

        row_buf[index, my_desc] = jnp.sum(racc_s[...].T, axis=0, keepdims=True)
        exchange("desc", n_desc, my_desc, row_buf, row_send, row_recv, index, between)
        return tree(jnp.add, [row_buf[index, p] for p in range(n_desc)])

    def col_sum(vector, v, index, w):
        def between():
            send_vec(v)
            window(w)
            run_tasks(3)

        def body(i, totals):
            for u in range(strips):
                at = pl.ds(pl.multiple_of((i * strips + u) * 8, 8), 8)
                here = vcol[at, :]
                totals = [totals[b] + plan[at, lane(b)] * here for b in range(blocks)]
            return totals

        vec_buf[v, 0] = vector
        spread_rows(vector)
        totals = lax.fori_loop(0, rows // (8 * strips), body, [jnp.zeros((8, LANES), F32)] * blocks)
        for b in range(blocks):
            col_buf[index, my_cell, :, lane(b)] = jnp.sum(totals[b], axis=0, keepdims=True)
        exchange("cell", n_cell, my_cell, col_buf, col_send, col_recv, index, between)
        return tree(jnp.add, [col_buf[index, p] for p in range(n_cell)])

    for k in range(1, ITERS):
        u_now = 1.0 / row_sum(k, 2)
        s_rows[k:k + 1, :] = u_now
        w_now = 1.0 / col_sum(u_now, k, k, k + 1)
        if k < ITERS - 1:
            t_rows[ITERS + 1 + k:ITERS + 2 + k, :] = w_now
            row_product(w_now)

    a_now = w_now * cg[...]
    for k in reversed(range(ITERS)):
        t = ITERS - 1 - k
        t_rows[k:k + 1, :] = a_now
        row_product(a_now)
        u_now = s_rows[k:k + 1, :]
        fbar = -(u_now * row_sum(ITERS + t, 2 if k > 0 else len(tasks) + 2 * n_cell))
        if k == ITERS - 1:
            fbar = fbar + cf[...]
        b_now = u_now * fbar
        s_rows[ITERS + k:ITERS + k + 1, :] = b_now
        if k > 0:
            w_before = t_rows[ITERS + k:ITERS + k + 1, :]
            a_now = -(w_before * (w_before * col_sum(b_now, ITERS + k, ITERS + t, ITERS + 1 + t)))
        else:
            vec_buf[ITERS, 0] = b_now
            send_vec(ITERS)

    pad = LANES - 2 * ITERS * len(PAIRS)

    def stack(value, which):
        parts = [part.astype(F32) for part in split3(value)]
        return jnp.concatenate([parts[pair[which]] for pair in PAIRS] + [jnp.zeros((pad, value.shape[1]), F32)], axis=0)

    s_cat[...] = stack(s_rows[...], 0).T.astype(BF16)
    t_cat[...] = stack(t_rows[...], 1).astype(BF16)

    x_chunk = rows // x_chunks
    levels = n_desc.bit_length() - 1

    def x_plan(chunk):
        steps, start, size, place = [], chunk * x_chunk, x_chunk, chunk * x_chunk
        for bit in range(levels):
            mine = lax.rem(my_desc // (1 << bit), 2)
            size = size // 2
            sent = start + (1 - mine) * size
            start = start + mine * size
            steps.append((flip(my_desc, 1 << bit), pl.multiple_of(sent, 8), pl.multiple_of(start, 8), size, place))
            place += size
        return steps

    plans = [x_plan(chunk) for chunk in range(x_chunks)]

    def x_scatter(chunk, level):
        peer, sent, kept, size, place = plans[chunk][level]
        return pltpu.make_async_remote_copy(
            src_ref=part_x.at[pl.ds(sent, size)],
            dst_ref=got_x.at[pl.ds(place, size)],
            send_sem=x_send.at[0, chunk, level],
            recv_sem=x_recv.at[0, chunk, level],
            device_id={"desc": peer},
            device_id_type=MESH,
        )

    def x_gather(chunk, level, arriving=False):
        peer, sent, kept, size, place = plans[chunk][level]
        at = pl.ds(sent if arriving else kept, size)
        return pltpu.make_async_remote_copy(
            src_ref=px.at[at],
            dst_ref=px.at[at],
            send_sem=x_send.at[1, chunk, level],
            recv_sem=x_recv.at[1, chunk, level],
            device_id={"desc": peer},
            device_id_type=MESH,
        )

    def x_add(chunk, level):
        peer, sent, kept, size, place = plans[chunk][level]
        x_scatter(chunk, level).wait_recv()
        out = part_x if level + 1 < levels else px
        out[pl.ds(kept, size), :] = part_x[pl.ds(kept, size), :] + got_x[pl.ds(place, size), :]
        if level + 1 < levels:
            x_scatter(chunk, level + 1).start()
        else:
            x_gather(chunk, level).start()

    def x_spread(chunk, level):
        x_gather(chunk, level, True).wait_recv()
        if level > 0:
            x_gather(chunk, level - 1).start()

    def x_make(at, slot):
        x_high[slot], x_low[slot] = split2(plan[at, :] * mm(s_cat[at, :], t_cat[...]))

    def x_use(at, slot):
        high, low = x_high[slot], x_low[slot]
        d_high, d_low = cat_d[:, :width], cat_d[:, width:2 * width]
        part_x[at, :] = (-scale) * (mm(high, d_high) + (mm(low, d_high) + mm(high, d_low)))

    def x_chunk_tiles(chunk):
        peer, sent, kept, size, place = plans[chunk][0]
        x_make(pl.ds(sent, size), 0)
        x_make(pl.ds(kept, size), 1)
        x_use(pl.ds(sent, size), 0)
        x_scatter(chunk, 0).start()
        x_use(pl.ds(kept, size), 1)

    down = [1 << bit for bit in reversed(range(n_cell.bit_length() - 1))]
    y_orders = [down[-1:] + down[:-1]] + [down] * (Y_CHUNKS - 1)
    y_starts = [y_block * eighth // 8 for eighth in (0, 1, 4, 6)]
    y_sizes = [y_block * eighth // 8 for eighth in (1, 3, 2, 2)]

    def y_after(chunk, rel):
        order = y_orders[chunk]
        return order[max([order.index(hop) + 1 for hop in order if rel & hop], default=0):]

    def y_copy(chunk, rel, arriving=False):
        hop = [hop for hop in y_orders[chunk] if rel & hop][-1]
        owner = flip(my_cell, rel if arriving else rel ^ hop)
        at = pl.ds(pl.multiple_of(owner * y_block + y_starts[chunk], 8), y_sizes[chunk])
        return pltpu.make_async_remote_copy(
            src_ref=py.at[at],
            dst_ref=py.at[at],
            send_sem=y_send.at[chunk, rel],
            recv_sem=y_recv.at[chunk, rel],
            device_id={"cell": flip(my_cell, hop)},
            device_id_type=MESH,
        )

    def y_pass(chunk, rel):
        if rel:
            y_copy(chunk, rel, True).wait_recv()
        for hop in y_after(chunk, rel):
            y_copy(chunk, rel | hop).start()

    def y_level(count, chunks):
        for chunk in chunks:
            for rel in sorted(range(n_cell), reverse=True):
                if bin(rel).count("1") == count:
                    y_pass(chunk, rel)

    x_chunk_tiles(0)

    for v in range(1, 2 * ITERS):
        for rel in range(1, n_cell):
            vec_copy(v, rel).wait_recv()
    t_part = stack(t_rows[:, my_slab], 1).T.astype(BF16)
    if not keep:
        far_cells[0] = cells[...]
    part = y_block // Y_PARTS
    part_chunks = Y_CHUNKS // Y_PARTS

    for rel in range(n_cell):
        s_here = jnp.concatenate(
            [jnp.ones((1, rows), F32)] + [vec_buf[v, rel] for v in range(1, 2 * ITERS)], axis=0
        )
        s_all[:, rel * rows:(rel + 1) * rows] = stack(s_here, 0).astype(BF16)

    for h in range(Y_PARTS):
        rows_here = slice(h * part, (h + 1) * part)
        sum_y[rows_here, :] = jnp.zeros((part, width), F32)

        def y_make(rel, slot):
            at = pl.ds(pl.multiple_of(rel * rows, rows), rows)
            high, low = split2(slab[rows_here, at] * mm(t_part[rows_here], s_all[:, at]))
            x_high[slot, rows_here, :rows], x_low[slot, rows_here, :rows] = high, low

        def y_use(rel, slot):
            at = pl.ds(pl.multiple_of(rel * rows, rows), rows)
            if keep:
                c_high, c_mid = keep_h[at, :], keep_m[at, :]
            else:
                c_high, c_mid = split2(far_cells[rel] * (scale * LOG2E))
            high, low = x_high[slot, rows_here, :rows], x_low[slot, rows_here, :rows]
            sum_y[rows_here, :] = sum_y[rows_here, :] + (mm(high, c_high) + (mm(low, c_high) + mm(high, c_mid)))

        def y_step(i, _):
            y_make(2 * i + 1, 1)
            y_use(2 * i, 0)
            y_make(jnp.minimum(2 * i + 2, n_cell - 1), 0)
            y_use(2 * i + 1, 1)
            return 0

        y_make(0, 0)
        lax.fori_loop(0, n_cell // 2, y_step, 0)
        py[pl.ds(pl.multiple_of(my_cell * y_block + h * part, part), part), :] = sum_y[rows_here, :] * (-1.0 / LOG2E)
        y_level(0, range(h * part_chunks, (h + 1) * part_chunks))
        if h == 0:
            for chunk in range(1):
                x_add(chunk, 0)
    for chunk in range(1, x_chunks):
        x_chunk_tiles(chunk)

    y_level(1, range(part_chunks))
    for chunk in range(1, x_chunks):
        x_add(chunk, 0)
    y_level(1, range(part_chunks, Y_CHUNKS))
    for level in range(1, levels):
        for chunk in range(x_chunks):
            x_add(chunk, level)
    y_level(2, range(part_chunks))
    for chunk in range(x_chunks):
        x_spread(chunk, levels - 1)
    y_level(2, range(part_chunks, Y_CHUNKS))
    for level in reversed(range(levels - 1)):
        for chunk in range(x_chunks):
            x_spread(chunk, level)
    for count in range(3, n_cell.bit_length()):
        y_level(count, range(Y_CHUNKS))

    for chunk in range(x_chunks):
        for level in range(levels):
            x_scatter(chunk, level).wait_send()
            x_gather(chunk, level).wait_send()
    for rel in range(1, n_cell):
        for chunk in range(Y_CHUNKS):
            y_copy(chunk, rel).wait_send()
        for p in range(PIECES):
            far_copy(p, rel).wait_send()
            swap_copy(p, rel, side).wait_send()
        for v in range(2 * ITERS):
            vec_copy(v, rel).wait_send()
    drain("desc", n_desc, my_desc, row_buf, row_send, row_recv, 2 * ITERS)
    drain("cell", n_cell, my_cell, col_buf, col_send, col_recv, 2 * ITERS - 1)


def run_plan(n_cell, n_desc, cells, descs, g_start, cot_f, cot_g):
    rows, width = cells.shape
    cols = descs.shape[0]
    vmem = pltpu.VMEM
    dma = pltpu.SemaphoreType.DMA
    spec = pl.BlockSpec(memory_space=pltpu.VMEM)
    n_row, n_col = 2 * ITERS, 2 * ITERS - 1
    x_levels = n_desc.bit_length() - 1
    kept, x_chunks = (n_cell * rows, 2) if n_cell <= 8 else (16, 4)
    return pl.pallas_call(
        functools.partial(plan_kernel, n_cell, n_desc),
        out_shape=(
            vmem((rows, width), F32),
            vmem((cols, width), F32),
        ),
        in_specs=[spec] * 5,
        out_specs=(spec, spec),
        scratch_shapes=[
            vmem((rows, cols), F32),
            vmem((rows, LANES), F32),
            vmem((rows, LANES), F32),
            vmem((8, cols), F32),
            vmem((8, cols), F32),
            vmem((8, cols), F32),
            vmem((cols, len(PAIRS) * width), BF16),
            vmem((2 * ITERS, rows), F32),
            vmem((2 * ITERS, cols), F32),
            vmem((1, cols), F32),
            vmem((rows, LANES), BF16),
            vmem((LANES, cols), BF16),
            vmem((2, rows // x_chunks // 2, cols), BF16),
            vmem((2, rows // x_chunks // 2, cols), BF16),
            vmem((n_row, n_desc, 1, rows), F32),
            vmem((n_col, n_cell, 1, cols), F32),
            dma((n_row, n_desc)),
            dma((n_row, n_desc)),
            dma((n_col, n_cell)),
            dma((n_col, n_cell)),
            vmem((rows, width), F32),
            vmem((rows, width), F32),
            dma((2, x_chunks, x_levels)),
            dma((2, x_chunks, x_levels)),
            vmem((n_cell, rows, width), F32),
            dma((PIECES, n_cell)),
            dma((PIECES, n_cell)),
            dma((PIECES, n_cell)),
            dma((PIECES, n_cell)),
            vmem((2 * ITERS, n_cell, 1, rows), F32),
            dma((2 * ITERS, n_cell)),
            dma((2 * ITERS, n_cell)),
            vmem((cols // n_cell, n_cell * rows), F32),
            vmem((cols // n_cell, LANES), F32),
            vmem((rows // 2, len(PAIRS) * width), BF16),
            vmem((kept, width), BF16),
            vmem((kept, width), BF16),
            vmem((LANES, n_cell * rows), BF16),
            vmem((cols // n_cell, width), F32),
            dma((Y_CHUNKS, n_cell)),
            dma((Y_CHUNKS, n_cell)),
        ],
        compiler_params=pltpu.CompilerParams(
            collective_id=0, has_side_effects=True, vmem_limit_bytes=60 * 1024 * 1024
        ),
        name="plan",
    )(cells, descs, g_start[None, :], cot_f[None, :], cot_g[None, :])


def solution(mesh):
    n_cell = mesh.shape["cell"]
    n_desc = mesh.shape["desc"]

    def on_device(cells, descs, g_start, cot_f, cot_g):
        return run_plan(n_cell, n_desc, cells, descs, g_start, cot_f, cot_g)

    placed = (P("cell", None), P("desc", None), P("desc"), P("cell"), P("desc"))
    return jax.shard_map(
        on_device,
        mesh=mesh,
        in_specs=placed,
        out_specs=(P("cell", None), P("desc", None)),
        check_vma=False,
    )
```
